128 devices in a mesh: circ: 8 (over z, y_hi), axial: 16 (over x, y_lo, core).
Axes of the slice: x: 4, y: 4 (y_hi: 2, y_lo: 2; y = y_hi * 2 + y_lo), z: 4, core: 2. Of those that a mesh axis runs over, the one named last changes fastest.
Arguments:
- position: float32 [3, 8, 16, 16384], P(None, 'circ', 'axial'), may hold values from -3 to 3
- displacement: float32 [3, 8, 16, 16384], P(None, 'circ', 'axial'), may hold values from -3 to 3
- velocity: float32 [3, 8, 16, 16384], P(None, 'circ', 'axial'), may hold values from -1.5 to 1.5
- bulk: float32 [8, 16, 16384], P('circ', 'axial'), may hold values from 6 to 30
- shear: float32 [8, 16, 16384], P('circ', 'axial'), may hold values from 0.5 to 2
- volume: float32 [8, 16, 16384], P('circ', 'axial'), may hold values from 60 to 200
- edges: int32 [8, 16, 2, 32], P('circ', 'axial'), may hold values from 0 to 127, as said below
- block_pairs: int32 [8, 16, 2, 320], P('circ', 'axial'), may hold values from 0 to 191, as said below
- block_counts: int32 [8, 16, 2], P('circ', 'axial'), may hold values from 128 to 320, as said below
- damage: int32 [8, 16, 320, 128, 128], P('circ', 'axial'), may hold values 0 or 1
Outputs:
- final_displacement: float32 [3, 8, 16, 16384], P(None, 'circ', 'axial')
- final_velocity: float32 [3, 8, 16, 16384], P(None, 'circ', 'axial')
- dilatation: float32 [8, 16, 16384], P('circ', 'axial')
The draws below stay inside these ranges and needn't reach their ends.
Inputs may be any that keep to these rules, and one draw needn't show every extreme that they name: `edges`: for each device the 64 entries are distinct clusters of that device. `block_pairs`: slot b below 128 pairs cluster b with itself; the further slots below block_counts[c, a, 0] pair two different clusters of the device; the next slots up to block_counts[c, a, 1] are cross blocks whose target is an extended slot of 128 or more, each extended slot of the device's neighbours used exactly once (only the circumferential ones on the last axial section); later slots hold unused pairs of two different local clusters. `block_counts`: entry 0 is the number of local blocks, 128 or more; entry 1 the number of all blocks of the device, which is 32 or 64 more than entry 0.
All inputs are finite; a program needn't handle non-finite values. No bound on the sum of `damage` on one device may be relied on, other than what follows from the above.
Results may differ from the reference program's by a relative error of at most 0.0003.
Values sent between devices are 32-bit elements; how exact they have to be, the bound alone decides.
No kernel may reach another device: no remote copies, remote signals or barrier semaphores. Data moves between devices by JAX's collectives and lax.ppermute only.
A program may use at most 64 MiB of HBM per device.

```python
import math
import jax
import jax.numpy as jnp
from jax import lax

CLUSTER_PTS = 128
CLUSTERS = 128
FACING = 32
GROUP_SLOTS = 16
TIME_STEPS = 2
BLOCK_SLOTS = 320
SECTORS = 8
SECTIONS = 16
POINTS_DEV = 16384


def draw_edges(key, part):
    device_keys = jax.random.split(jax.random.fold_in(key, 3), SECTORS * SECTIONS)

    def one_device(device_key):
        order = jax.random.permutation(device_key, CLUSTERS).astype(jnp.int32)
        return order[:2 * FACING].reshape(2, FACING)
    return jax.vmap(one_device)(device_keys).reshape(SECTORS, SECTIONS, 2, FACING)


def block_layout(key):
    base_key = jax.random.fold_in(key, 7)
    crack_key, count_key, pair_key = jax.random.split(base_key, 3)
    crack_circ = jax.random.randint(crack_key, (), 0, SECTORS)
    crack_axial = jax.random.randint(jax.random.fold_in(crack_key, 1), (), 0, SECTIONS)
    circ_index = jnp.arange(SECTORS, dtype=jnp.int32)[:, None]
    axial_index = jnp.arange(SECTIONS, dtype=jnp.int32)[None, :]
    in_crack = ((circ_index - crack_circ) % SECTORS <= 1) & (jnp.abs(axial_index - crack_axial) <= SECTIONS // 4)
    last_section = (axial_index == SECTIONS - 1) & (circ_index >= 0)
    cross_count = jnp.where(last_section, FACING, 2 * FACING)
    quiet = CLUSTERS + jax.random.randint(count_key, (SECTORS, SECTIONS), CLUSTERS // 4, CLUSTERS // 2 + 1)
    local_count = jnp.where(in_crack, BLOCK_SLOTS - cross_count, quiet).astype(jnp.int32)
    total_count = (local_count + cross_count).astype(jnp.int32)
    device_keys = jax.random.split(pair_key, SECTORS * SECTIONS)

    def one_device(device_key, local_number, is_last):
        order_key, offset_key, source_key, both_key, circ_key = jax.random.split(device_key, 5)
        slot_index = jnp.arange(BLOCK_SLOTS, dtype=jnp.int32)
        order = jax.random.permutation(order_key, CLUSTERS).astype(jnp.int32)
        offsets = jax.random.randint(offset_key, (BLOCK_SLOTS,), 1, 4).astype(jnp.int32)
        extra_index = jnp.maximum(slot_index - CLUSTERS, 0) % CLUSTERS
        extra_source = order[extra_index]
        is_self = slot_index < CLUSTERS
        local_source = jnp.where(is_self, slot_index, extra_source)
        local_target = jnp.where(is_self, slot_index, (extra_source + offsets) % CLUSTERS)
        cross_sources = jax.random.permutation(source_key, CLUSTERS).astype(jnp.int32)
        both_order = jax.random.permutation(both_key, 2 * FACING).astype(jnp.int32)
        circ_order = jax.random.permutation(circ_key, FACING).astype(jnp.int32)
        cross_slot = slot_index - local_number
        crossing = (cross_slot >= 0) & (cross_slot < jnp.where(is_last, FACING, 2 * FACING))
        picked = jnp.where(is_last, circ_order[jnp.clip(cross_slot, 0, FACING - 1)], both_order[jnp.clip(cross_slot, 0, 2 * FACING - 1)])
        source_ids = jnp.where(crossing, cross_sources[jnp.clip(cross_slot, 0, CLUSTERS - 1)], local_source)
        target_ids = jnp.where(crossing, CLUSTERS + picked, local_target)
        return jnp.stack([source_ids, target_ids]).astype(jnp.int32)
    pairs = jax.vmap(one_device)(device_keys, local_count.reshape(-1), last_section.reshape(-1))
    return (local_count, total_count, pairs.reshape(SECTORS, SECTIONS, 2, BLOCK_SLOTS))


def draw_block_pairs(key, part):
    return block_layout(key)[2]


def draw_block_counts(key, part):
    local_count, total_count, pairs = block_layout(key)
    return jnp.stack([local_count, total_count], axis=-1).astype(jnp.int32)


def plant(array, stream_key, smallest, high):
    index_at = [jax.random.randint(jax.random.fold_in(stream_key, axis), (), 0, length) for axis, length in enumerate(array.shape)]
    widest = array.shape.index(max(array.shape))
    beside = index_at[:widest] + [(index_at[widest] + 1) % array.shape[widest]] + index_at[widest + 1:]
    return array.at[tuple(index_at)].set(smallest).at[tuple(beside)].set(high)


def shard_levels(rng, shape, shards, least, top_value):
    factor_of = 1.0
    for axis_at, blocks in shards:
        draws = jax.random.uniform(jax.random.fold_in(jax.random.fold_in(rng, 6), axis_at), (blocks,), jnp.float32, least / len(shards), top_value / len(shards))
        factor_of = factor_of * jnp.repeat(jnp.exp(draws), shape[axis_at] // blocks).reshape((-1,) + (1,) * (len(shape) - 1 - axis_at))
    return factor_of


def centred(stream_key, dims, deviation, most, pieces=(), kind=jnp.bfloat16):
    gain = shard_levels(stream_key, dims, pieces, -0.22, 0.18) if pieces else 1.0
    drawn = jax.random.normal(stream_key, dims, jnp.float32) * deviation * gain
    return jnp.minimum(jnp.maximum(drawn, -most), most).astype(kind)


def setup_inputs(seed: int = 0) -> dict:
    arg_keys = jax.random.split(jax.random.key(seed), 11)
    return {
        "position": centred(arg_keys[0], (3, SECTORS, SECTIONS, POINTS_DEV), 0.5, 3.0, ((1, 8), (2, 16)), jnp.float32),
        "displacement": centred(arg_keys[1], (3, SECTORS, SECTIONS, POINTS_DEV), 0.5, 3.0, ((1, 8), (2, 16)), jnp.float32),
        "velocity": centred(arg_keys[2], (3, SECTORS, SECTIONS, POINTS_DEV), 0.2, 1.5, ((1, 8), (2, 16)), jnp.float32),
        "bulk": jnp.clip(jnp.exp(math.log(30.0) - 1.609438 * jax.random.uniform(arg_keys[3], (SECTORS, SECTIONS, POINTS_DEV), jnp.float32) ** shard_levels(arg_keys[3], (SECTORS, SECTIONS, POINTS_DEV), ((0, 8), (1, 16)), -0.2, 0.2)), 6.0, 30.0),
        "shear": jnp.clip(jnp.exp(math.log(2.0) - 1.3862944 * jax.random.uniform(arg_keys[4], (SECTORS, SECTIONS, POINTS_DEV), jnp.float32) ** shard_levels(arg_keys[4], (SECTORS, SECTIONS, POINTS_DEV), ((0, 8), (1, 16)), -0.2, 0.2)), 0.5, 2.0),
        "volume": jnp.clip(jnp.exp(math.log(200.0) - 1.2039728 * jax.random.uniform(arg_keys[5], (SECTORS, SECTIONS, POINTS_DEV), jnp.float32) ** shard_levels(arg_keys[5], (SECTORS, SECTIONS, POINTS_DEV), ((0, 8), (1, 16)), -0.2, 0.2)), 60.0, 200.0),
        "edges": draw_edges(jax.random.fold_in(arg_keys[10], 71), 0),
        "block_pairs": draw_block_pairs(jax.random.fold_in(arg_keys[10], 71), 0),
        "block_counts": draw_block_counts(jax.random.fold_in(arg_keys[10], 71), 0),
        "damage": plant((jax.random.randint(arg_keys[9], (SECTORS, SECTIONS, BLOCK_SLOTS, CLUSTER_PTS, CLUSTER_PTS), 0, 20) < 17).astype(jnp.int32), jax.random.fold_in(arg_keys[9], 1), 0, 1),
    }


SOFTEN = 0.01
HORIZON_SQ = 1.0
TIMESTEP = 0.07

def bond_geometry(source, target):
    spacing = target[:, 0:3, None, :] - source[:, 0:3, :, None]
    relative = target[:, 3:6, None, :] - source[:, 3:6, :, None]
    stretched = spacing + relative
    length_sq = lax.optimization_barrier(jnp.sum(spacing * spacing, axis=1))
    deformed_sq = lax.optimization_barrier(jnp.sum(stretched * stretched, axis=1))
    length = jnp.sqrt(length_sq)
    extension = jnp.sqrt(deformed_sq) - length
    influence = jnp.exp(-length_sq / HORIZON_SQ)
    return (stretched, deformed_sq, length, extension, influence)

def bond_pass(source, target, weight, phase_no):
    stretched, deformed_sq, length, extension, influence = bond_geometry(source, target)
    if phase_no == 1:
        bond_term = weight * influence * length * extension
        return (lax.optimization_barrier(jnp.sum(bond_term, axis=2))[:, None, :], lax.optimization_barrier(jnp.sum(bond_term, axis=1))[:, None, :])
    own_state = influence * (source[:, 6, :, None] * source[:, 8, :, None] * length + source[:, 7, :, None] * extension)
    other_state = influence * (target[:, 6, None, :] * target[:, 8, None, :] * length + target[:, 7, None, :] * extension)
    magnitude = weight * (own_state + other_state) / jnp.sqrt(deformed_sq + SOFTEN)
    bond_force = magnitude[:, None] * stretched
    return (lax.optimization_barrier(jnp.sum(bond_force, axis=3)), -lax.optimization_barrier(jnp.sum(bond_force, axis=2)))

def bond_weight(source_ids, target_ids, usable, damage_slab):
    points = damage_slab.shape[-1]
    upper_tri = lax.broadcasted_iota(jnp.int32, (points, points), 0) < lax.broadcasted_iota(jnp.int32, (points, points), 1)
    keeper = jnp.where((source_ids == target_ids)[:, None, None], upper_tri[None], True)
    keeper = keeper & usable[:, None, None]
    return jnp.where(keeper, damage_slab.astype(jnp.float32), jnp.zeros(damage_slab.shape, jnp.float32))

def device_pass(inputs, phase_no, row_width):
    point_table, source_list, target_list, total_count, damage_all = inputs
    extent = point_table.shape[0]

    def turn(group_index, accumulated):
        first_slot = group_index * GROUP_SLOTS
        slot_ids = first_slot + jnp.arange(GROUP_SLOTS, dtype=jnp.int32)
        usable = slot_ids < total_count
        source_ids = jnp.where(usable, lax.dynamic_slice_in_dim(source_list, first_slot, GROUP_SLOTS), 0)
        target_ids = jnp.where(usable, lax.dynamic_slice_in_dim(target_list, first_slot, GROUP_SLOTS), 0)
        damage_slab = lax.dynamic_slice_in_dim(damage_all, first_slot, GROUP_SLOTS)
        weight = bond_weight(source_ids, target_ids, usable, damage_slab)
        source_part, target_part = bond_pass(point_table[source_ids], point_table[target_ids], weight, phase_no)
        return accumulated.at[source_ids].add(source_part).at[target_ids].add(target_part)
    empty = jnp.zeros((extent, row_width, point_table.shape[-1]), jnp.float32)
    return lax.fori_loop(0, (total_count + GROUP_SLOTS - 1) // GROUP_SLOTS, turn, empty)

def all_devices(full_table, source_lists, target_lists, totals, slabs, phase_no, row_width):
    devices = SECTORS * SECTIONS
    flat_table = full_table.reshape((devices,) + full_table.shape[2:])
    result = lax.map(lambda inputs: device_pass(inputs, phase_no, row_width), (flat_table, source_lists, target_lists, totals, slabs))
    return result.reshape((SECTORS, SECTIONS) + result.shape[1:])

def clustered(quantity):
    row_count = quantity.shape[0]
    shaped = quantity.reshape(row_count, SECTORS, SECTIONS, CLUSTERS, CLUSTER_PTS)
    return jnp.transpose(shaped, (1, 2, 3, 0, 4))

def flattened(quantity):
    row_count = quantity.shape[3]
    return jnp.transpose(quantity, (3, 0, 1, 2, 4)).reshape(row_count, SECTORS, SECTIONS, POINTS_DEV)

def facing(stacked, edges):
    upper_rows = jnp.roll(stacked, -1, axis=0)
    upper_ids = jnp.roll(edges[:, :, 0], -1, axis=0)
    after_rows = jnp.concatenate([stacked[:, 1:], jnp.zeros_like(stacked[:, :1])], axis=1)
    after_ids = jnp.concatenate([edges[:, 1:, 1], jnp.zeros_like(edges[:, :1, 1])], axis=1)
    shape_out = upper_ids.shape + stacked.shape[3:]
    upward = jnp.take_along_axis(upper_rows, jnp.broadcast_to(upper_ids[:, :, :, None, None], shape_out), axis=2)
    axially = jnp.take_along_axis(after_rows, jnp.broadcast_to(after_ids[:, :, :, None, None], shape_out), axis=2)
    return (upward, axially)

def returned(partials, edges):
    local_part = partials[:, :, :CLUSTERS]
    upward = jnp.roll(partials[:, :, CLUSTERS:CLUSTERS + FACING], 1, axis=0)
    before = partials[:, :, CLUSTERS + FACING:]
    axially = jnp.concatenate([jnp.zeros_like(before[:, :1]), before[:, :-1]], axis=1)
    cluster_ids = jnp.arange(CLUSTERS, dtype=jnp.int32)
    circ_hot = (edges[:, :, 0, :, None] == cluster_ids).astype(jnp.float32)
    axial_hot = (edges[:, :, 1, :, None] == cluster_ids).astype(jnp.float32)
    from_upper = jnp.einsum('safk,safrc->sakrc', circ_hot, upward, precision=lax.Precision.HIGHEST)
    from_after = jnp.einsum('safk,safrc->sakrc', axial_hot, axially, precision=lax.Precision.HIGHEST)
    return local_part + from_upper + from_after

def reference(position, displacement, velocity, bulk, shear, volume, edges, block_pairs, block_counts, damage):
    point_positions = clustered(position)
    moving_state = clustered(displacement)
    velocities = clustered(velocity)
    bulk_modulus = clustered(bulk[None])
    shear_modulus = clustered(shear[None])
    weighted_volume = clustered(volume[None])
    dilatation_factor = (3.0 * bulk_modulus - 5.0 * shear_modulus) / weighted_volume
    deviatoric_factor = 15.0 * shear_modulus / weighted_volume
    devices = SECTORS * SECTIONS
    pair_lists = block_pairs.reshape(devices, 2, BLOCK_SLOTS)
    totals = block_counts[:, :, 1].reshape(devices)
    slabs = damage.reshape(devices, BLOCK_SLOTS, CLUSTER_PTS, CLUSTER_PTS)
    dilatation = jnp.zeros_like(weighted_volume)
    for step_index in range(TIME_STEPS):
        first_table = jnp.concatenate([point_positions, moving_state], axis=3)
        upward, axially = facing(first_table, edges)
        full_table = jnp.concatenate([first_table, upward, axially], axis=2)
        partials = all_devices(full_table, pair_lists[:, 0], pair_lists[:, 1], totals, slabs, 1, 1)
        dilatation = 3.0 * returned(partials, edges) / weighted_volume
        second_point_table = jnp.concatenate([point_positions, moving_state, dilatation_factor, deviatoric_factor, dilatation], axis=3)
        upward, axially = facing(second_point_table, edges)
        full_table = jnp.concatenate([second_point_table, upward, axially], axis=2)
        partials = all_devices(full_table, pair_lists[:, 0], pair_lists[:, 1], totals, slabs, 2, 3)
        force = returned(partials, edges)
        velocities = velocities + TIMESTEP * force
        moving_state = moving_state + TIMESTEP * velocities
    return (flattened(moving_state), flattened(velocities), flattened(dilatation)[0])
```

```python
import functools

import jax
import jax.numpy as jnp
from jax import lax
from jax.experimental import pallas as pl
from jax.experimental.pallas import tpu as pltpu
from jax.sharding import PartitionSpec as P

PTS = 128
CL = 128
FACING = 32
EXT = CL + 2 * FACING
SLOTS = 320
STEPS = 2
TIMESTEP = 0.07
SOFTEN = 0.01
LOG2E = 1.4426950408889634
KAPPA = LOG2E**0.5
TINY = 1e-30
GROUP = 16
UNROLL = 8
OWN = CL * PTS
GHOST = FACING * PTS
F32 = jnp.float32
BF16 = jnp.bfloat16
NT = (((1,), (1,)), ((), ()))
NN = (((1,), (0,)), ((), ()))


def lanes(c):
    return pl.ds(pl.multiple_of(c * PTS, PTS), PTS)


def dot(a, b, dims):
    return lax.dot_general(a, b, dims, preferred_element_type=F32)


def split3(x):
    h = x.astype(BF16).astype(F32)
    rest = x - h
    m = rest.astype(BF16).astype(F32)
    return h, m, rest - m


def hilo(x):
    h = x.astype(BF16)
    return h, (x - h.astype(F32)).astype(BF16)


def rows8():
    return lax.broadcasted_iota(jnp.int32, (8, PTS), 0)


def coordinate_parts(s):
    row = rows8()
    sq = s * s
    nx = sq[0:1] + sq[1:2] + sq[2:3]
    ny = sq[4:5] + sq[5:6] + sq[6:7]
    full = jnp.where(row == 3, nx, jnp.where(row == 7, ny, s))
    return split3(full)


def source_features(parts):
    p0, p1, p2 = parts
    one = jnp.ones((8, PTS), F32)
    stack = jnp.concatenate([p0, p0, p0, p1, p1, p2, one, one], axis=0)
    return jnp.transpose(stack).astype(BF16)


def target_features(parts):
    p0, p1, p2 = parts
    row = rows8()
    norm = (row == 3) | (row == 7)
    a0 = jnp.where(norm, -1.0, 2.0 * p0)
    a1 = jnp.where(norm, 0.0, 2.0 * p1)
    a2 = jnp.where(norm, 0.0, 2.0 * p2)
    n0 = jnp.where(norm, -p0, 0.0)
    shifted = pltpu.roll(p2, 1, 0)
    n1 = jnp.where(norm, -p1, 0.0)
    upper = row < 4
    after = (row == 4) | (row == 0)
    stack = jnp.concatenate([a0, a1, a2, a0, a1, a0], axis=0)
    up6 = jnp.concatenate([upper] * 6, axis=0)

    def half(top):
        keep = up6 if top else ~up6
        body = jnp.where(keep, stack, 0.0)
        near = upper if top else ~upper
        tail0 = jnp.where(near, n0, 0.0)
        tail1 = jnp.where(near, n1, 0.0) - jnp.where(row == (4 if top else 0), shifted, 0.0)
        return jnp.concatenate([body, tail0, tail1], axis=0).astype(BF16)

    return half(True), half(False)


def moment_features(parts):
    p0, p1, p2 = parts
    row = rows8()
    first = jnp.where(row == 3, 1.0, jnp.where(row > 3, p0, 0.0))
    first = jnp.where(row == 7, 0.0, first)
    second = jnp.where((row > 3) & (row < 7), p1, 0.0) + jnp.where(
        row < 3, pltpu.roll(p2, 4, 0), 0.0
    )
    m = jnp.concatenate([first, second], axis=0).astype(BF16)
    return jnp.concatenate([m, m], axis=1)


def pack_kernel(edges, x_ref, u_ref, v_ref, bulk, shear, volume, s_out, v_out, mean, send_c, send_a):
    chunk = 2048
    zero = jnp.zeros((1, chunk), F32)

    def turn(i, total):
        sl = pl.ds(pl.multiple_of(i * chunk, chunk), chunk)
        x = KAPPA * x_ref[:, sl]
        y = x + KAPPA * u_ref[:, sl]
        s = jnp.concatenate([x, zero, y, zero], axis=0)
        s_out[:, sl] = s
        vol = volume[:, sl]
        mu = shear[:, sl]
        dil = (3.0 * bulk[:, sl] - 5.0 * mu) / vol
        dev = 15.0 * mu / vol
        thr = (3.0 / LOG2E) / vol
        v_out[:, sl] = jnp.concatenate([dil, dev, thr, zero, KAPPA * v_ref[:, sl], zero], axis=0)
        return total + jnp.sum(s, axis=1, keepdims=True)

    total = lax.fori_loop(0, OWN // chunk, turn, jnp.zeros((8, 1), F32))
    mean[...] = jnp.broadcast_to(total * (1.0 / OWN), (8, PTS))

    def copy(f, _):
        for side, out in ((0, send_c), (1, send_a)):
            e = edges[side, f]
            out[0:8, lanes(f)] = s_out[:, lanes(e)]
            out[8:16, lanes(f)] = v_out[:, lanes(e)]
        return 0

    lax.fori_loop(0, FACING, copy, 0, unroll=4)


def each_cluster(own, ghost_c, ghost_a, fn, unroll):
    lax.fori_loop(0, CL, lambda c, _: (fn(c, own[:, lanes(c)]), 0)[1], 0, unroll=unroll)
    lax.fori_loop(
        0, FACING, lambda c, _: (fn(CL + c, ghost_c[:, lanes(c)]), 0)[1], 0, unroll=unroll
    )
    lax.fori_loop(
        0,
        FACING,
        lambda c, _: (fn(CL + FACING + c, ghost_a[:, lanes(c)]), 0)[1],
        0,
        unroll=unroll,
    )


def build_geometry(c, s, left, right, moments):
    parts = coordinate_parts(s)
    if left is not None:
        left[jnp.minimum(c, CL)] = source_features(parts)
    t0, t1 = target_features(parts)
    right[c, :, 0:PTS] = t0
    right[c, :, PTS:] = t1
    if moments is not None:
        moments[c] = moment_features(parts)


def slot_ids(pairs, counts, slot):
    p = pairs[0, slot]
    q = pairs[1, slot]
    live = slot < counts[1]
    return p, q, jnp.where(live, p, EXT), jnp.where(live, q, EXT)


def for_groups(counts, one_turn):
    g = pl.program_id(0)

    @pl.when(g * GROUP < counts[1])
    def _():
        def turn(i, _):
            one_turn(g * GROUP + i * UNROLL, i * UNROLL)
            return 0

        lax.fori_loop(0, GROUP // UNROLL, turn, 0)


def first_sums(pairs, counts, base, inner, weight_of, left, right, acc):
    ones = jnp.ones((16, 2 * PTS), BF16)
    found = []
    for j in range(UNROLL):
        p, q, pa, qa = slot_ids(pairs, counts, base + j)
        ab = dot(left[p], right[q], NN)
        na = ab[:, :PTS]
        nb = ab[:, PTS:]
        w = weight_of(na, inner + j, base + j)
        x = jnp.maximum(na * nb, TINY)
        t = (x * lax.rsqrt(x) + na) * w
        h, l = hilo(t)
        both_q = dot(ones, jnp.concatenate([h, l], axis=0), NN)
        both_p = dot(ones, jnp.concatenate([h, l], axis=1), NT)
        found.append((pa, qa, both_p, both_q))
    for pa, qa, gp, gq in found:
        acc[qa] += gq[0:8]
        acc[pa] += gp[0:8]


def send_rows(edges, acc_row, own_out, gc_out, ga_out, send_c, send_a):
    def own(c, _):
        own_out[:, lanes(c)] = acc_row(c)
        return 0

    lax.fori_loop(0, CL, own, 0, unroll=4)

    def ghost(f, _):
        gc_out[:, lanes(f)] = acc_row(CL + f)
        ga_out[:, lanes(f)] = acc_row(CL + FACING + f)
        send_c[:, lanes(f)] = acc_row(edges[0, f])
        send_a[:, lanes(f)] = acc_row(edges[1, f])
        return 0

    lax.fori_loop(0, FACING, ghost, 0, unroll=4)


def zero_acc(acc):
    acc[...] = jnp.zeros_like(acc)


def dilatation_first(
    pairs, counts, edges, s_own, s_c, s_a, mean, damage,
    w_out, n_own, n_c, n_a, send_c, send_a,
    left, right, acc, cut,
):
    g = pl.program_id(0)

    @pl.when(g == 0)
    def _():
        zero_acc(acc)
        i0 = lax.broadcasted_iota(jnp.int32, (PTS, PTS), 0)
        i1 = lax.broadcasted_iota(jnp.int32, (PTS, PTS), 1)
        cut[0] = jnp.where(i0 < i1, 0, 1)
        cut[1] = jnp.zeros((PTS, PTS), jnp.int32)
        shift = mean[...]
        fn = lambda c, s: build_geometry(c, s[0:8] - shift, left, right, None)
        each_cluster(s_own, s_c, s_a, fn, 2)

    def weight_of(na, k, slot):
        keep = damage[k] > cut[jnp.where(slot < CL, 0, 1)]
        w = jnp.where(keep, jnp.exp2(na), 0.0)
        w_out[k] = w
        return w

    for_groups(
        counts,
        lambda base, inner: first_sums(pairs, counts, base, inner, weight_of, left, right, acc),
    )

    @pl.when(g == pl.num_programs(0) - 1)
    def _():
        row = lambda c: acc[c, 0:1, :]
        send_rows(edges, row, n_own, n_c, n_a, send_c, send_a)


def dilatation_again(
    pairs, counts, edges, s_own, s_c, s_a, v_own, v_c, v_a, mean, f_own, f_c, f_a,
    up_c, up_a, back_c, back_a, weights,
    s_own2, s_c2, s_a2, v_own2, v_c2, v_a2, n_own, n_c, n_a, send_c, send_a,
    left, right, acc,
):
    g = pl.program_id(0)

    @pl.when(g == 0)
    def _():
        zero_acc(acc)
        advance(edges, s_own, s_c, s_a, v_own, v_c, v_a, f_own, f_c, f_a, up_c, up_a, back_c,
                back_a, s_own2, s_c2, s_a2, v_own2, v_c2, v_a2)
        shift = mean[...]
        fn = lambda c, s: build_geometry(c, s[0:8] - shift, left, right, None)
        each_cluster(s_own2, s_c2, s_a2, fn, 2)

    weight_of = lambda na, k, slot: weights[k]
    for_groups(
        counts,
        lambda base, inner: first_sums(pairs, counts, base, inner, weight_of, left, right, acc),
    )

    @pl.when(g == pl.num_programs(0) - 1)
    def _():
        row = lambda c: acc[c, 0:1, :]
        send_rows(edges, row, n_own, n_c, n_a, send_c, send_a)


def advance(edges, s_own, s_c, s_a, v_own, v_c, v_a, f_own, f_c, f_a, up_c, up_a, back_c, back_a,
            s_own2, s_c2, s_a2, v_own2, v_c2, v_a2):
    pad = jnp.zeros((4, PTS), F32)

    def moved(s, v, f):
        f8 = jnp.concatenate([pad, f], axis=0)
        v2 = v + TIMESTEP * f8
        keep = rows8() < 4
        return s + jnp.where(keep, 0.0, TIMESTEP * v2), v2

    def own(c, _):
        s2, v2 = moved(s_own[:, lanes(c)], v_own[:, lanes(c)], f_own[:, lanes(c)])
        s_own2[:, lanes(c)] = s2
        v_own2[:, lanes(c)] = v2
        return 0

    lax.fori_loop(0, CL, own, 0, unroll=4)

    def ghost(f, _):
        for side, back in ((0, back_c), (1, back_a)):
            e = edges[side, f]
            total = f_own[:, lanes(e)] + back[:, lanes(f)]
            s2, v2 = moved(s_own[:, lanes(e)], v_own[:, lanes(e)], total)
            s_own2[:, lanes(e)] = s2
            v_own2[:, lanes(e)] = v2
        for s, v, part, up, s_out, v_out in (
            (s_c, v_c, f_c, up_c, s_c2, v_c2),
            (s_a, v_a, f_a, up_a, s_a2, v_a2),
        ):
            total = up[:, lanes(f)] + part[:, lanes(f)]
            s2, v2 = moved(s[0:8, lanes(f)], v[:, lanes(f)], total)
            s_out[:, lanes(f)] = s2
            v_out[:, lanes(f)] = v2
        return 0

    lax.fori_loop(0, FACING, ghost, 0, unroll=2)


def force_pass(
    pairs, counts, edges, s_own, s_c, s_a, v_own, v_c, v_a, mean, n_own, n_c, n_a,
    up_c, up_a, back_c, back_a, weights,
    theta_out, f_own, f_c, f_a, send_c, send_a,
    left, right, moments, acc, n_full, coef_row, coef_col,
):
    g = pl.program_id(0)

    @pl.when(g == 0)
    def _():
        zero_acc(acc)
        shift = mean[...]
        fn = lambda c, s: build_geometry(c, s[0:8] - shift, left, right, moments)
        each_cluster(s_own, s_c, s_a, fn, 2)
        n_full[:, 0:OWN] = n_own[...]

        def mend(f, _):
            n_full[:, lanes(edges[0, f])] = n_own[:, lanes(edges[0, f])] + back_c[:, lanes(f)]
            n_full[:, lanes(edges[1, f])] = n_own[:, lanes(edges[1, f])] + back_a[:, lanes(f)]
            n_full[:, lanes(CL + f)] = up_c[:, lanes(f)] + n_c[:, lanes(f)]
            n_full[:, lanes(CL + FACING + f)] = up_a[:, lanes(f)] + n_a[:, lanes(f)]
            return 0

        lax.fori_loop(0, FACING, mend, 0, unroll=4)

        def coefs(c, v):
            theta = v[2:3] * n_full[:, lanes(c)]
            dev = v[1:2]
            minus = dev - v[0:1] * theta
            row = jnp.concatenate([minus, -dev, theta, jnp.zeros((5, PTS), F32)], axis=0)
            coef_row[c] = row
            return row

        def own(c, _):
            row = coefs(c, v_own[:, lanes(c)])
            theta_out[:, lanes(c)] = row[2:3]
            coef_col[c] = jnp.transpose(row)
            return 0

        lax.fori_loop(0, CL, own, 0, unroll=4)

        def ghost(f, _):
            coefs(CL + f, v_c[:, lanes(f)])
            coefs(CL + FACING + f, v_a[:, lanes(f)])
            return 0

        lax.fori_loop(0, FACING, ghost, 0, unroll=4)

    def turn(base, inner):
        found = []
        for j in range(UNROLL):
            p, q, pa, qa = slot_ids(pairs, counts, base + j)
            ab = dot(left[p], right[q], NN)
            na = jnp.minimum(ab[:, :PTS], -TINY)
            nb = jnp.minimum(ab[:, PTS:], -TINY)
            nu = nb - SOFTEN * LOG2E
            col = coef_col[p]
            row = coef_row[q]
            mc = jnp.broadcast_to(col[:, 0:1], (PTS, PTS)) + row[0:1]
            mb = jnp.broadcast_to(col[:, 1:2], (PTS, PTS)) + row[1:2]
            za = na * lax.rsqrt(na * nu)
            zb = nb * lax.rsqrt(nb * nu)
            m = weights[inner + j] * (mc * za + mb * zb)
            h, l = hilo(m)
            gq = dot(moments[p], jnp.concatenate([h, l], axis=0), NN)
            gp = dot(moments[q], jnp.concatenate([h, l], axis=1), NT)
            found.append((pa, qa, gp, gq))
        for pa, qa, gp, gq in found:
            acc[qa] += gq
            acc[pa] += gp

    for_groups(counts, turn)

    @pl.when(g == pl.num_programs(0) - 1)
    def _():
        shift = mean[...]

        def force(c, s):
            gsum = acc[c]
            first, second = gsum[0:8], gsum[8:16]
            y = s[0:8] - shift
            total = first + second + pltpu.roll(second, 4, 0)
            return (total - y * first[3:4])[4:8]

        def own(c, _):
            f_own[:, lanes(c)] = force(c, s_own[:, lanes(c)])
            return 0

        lax.fori_loop(0, CL, own, 0, unroll=4)

        def ghost(f, _):
            f_c[:, lanes(f)] = force(CL + f, s_c[0:8, lanes(f)])
            f_a[:, lanes(f)] = force(CL + FACING + f, s_a[0:8, lanes(f)])
            send_c[:, lanes(f)] = f_own[:, lanes(edges[0, f])]
            send_a[:, lanes(f)] = f_own[:, lanes(edges[1, f])]
            return 0

        lax.fori_loop(0, FACING, ghost, 0, unroll=4)


def finish_kernel(edges, u_ref, s_start, s_own, v_own, f_own, back_c, back_a, u_out, vel_out):
    chunk = 2048

    def turn(i, _):
        sl = pl.ds(pl.multiple_of(i * chunk, chunk), chunk)
        v2 = v_own[4:7, sl] + TIMESTEP * f_own[0:3, sl]
        vel_out[:, sl] = v2 * (1.0 / KAPPA)
        gone = (s_own[4:7, sl] - s_start[4:7, sl]) + TIMESTEP * v2
        u_out[:, sl] = u_ref[:, sl] + gone * (1.0 / KAPPA)
        return 0

    lax.fori_loop(0, OWN // chunk, turn, 0)

    def mend(f, _):
        for side, back in ((0, back_c), (1, back_a)):
            sl = lanes(edges[side, f])
            more = (TIMESTEP / KAPPA) * back[0:3, lanes(f)]
            vel_out[:, sl] = vel_out[:, sl] + more
            u_out[:, sl] = u_out[:, sl] + TIMESTEP * more
        return 0

    lax.fori_loop(0, FACING, mend, 0, unroll=4)


SMEM = pl.BlockSpec(memory_space=pltpu.SMEM)
VMEM = pl.BlockSpec(memory_space=pltpu.VMEM)


def table(rows, n):
    return jax.ShapeDtypeStruct((rows, n), F32)


def slab_spec():
    def index(g, pairs, counts):
        return (jnp.minimum(g, (counts[1] - 1) // GROUP), 0, 0)

    return pl.BlockSpec((GROUP, PTS, PTS), index)


def sweep(kernel, name, pairs, counts, edges, tables, slab, out_tables, scratch, slab_out=None):
    spec = lambda *shape: pl.BlockSpec(shape, lambda g, a, b: (0, 0))
    whole = [pl.BlockSpec(x.shape, lambda g, a, b: (0, 0), pipeline_mode=pl.Buffered(1)) for x in tables]
    outs = [spec(*x.shape) for x in out_tables]
    out_shape = list(out_tables)
    if slab_out is not None:
        outs = [slab_spec()] + outs
        out_shape = [slab_out] + out_shape
    return pl.pallas_call(
        kernel,
        out_shape=out_shape,
        grid_spec=pltpu.PrefetchScalarGridSpec(
            num_scalar_prefetch=2,
            grid=(SLOTS // GROUP,),
            in_specs=[SMEM] + whole + [slab_spec()],
            out_specs=outs,
            scratch_shapes=scratch,
        ),
        compiler_params=pltpu.CompilerParams(
            dimension_semantics=("arbitrary",), vmem_limit_bytes=56 << 20
        ),
        name=name,
    )(pairs, counts, edges, *tables, slab)


LEFT = pltpu.VMEM((CL + 1, PTS, 64), BF16)
RIGHT = pltpu.VMEM((EXT, 64, 2 * PTS), BF16)
N_TABLES = [table(1, OWN)] + [table(1, GHOST)] * 4
F_TABLES = [table(4, OWN)] + [table(4, GHOST)] * 4


def run_first(pairs, counts, edges, s_own, s_c, s_a, mean, damage):
    return sweep(
        dilatation_first, "dil0", pairs, counts, edges, [s_own, s_c, s_a, mean], damage, N_TABLES,
        [LEFT, RIGHT, pltpu.VMEM((EXT + 1, 8, PTS), F32), pltpu.VMEM((2, PTS, PTS), jnp.int32)],
        slab_out=jax.ShapeDtypeStruct((SLOTS, PTS, PTS), F32),
    )


def run_again(pairs, counts, edges, tables, weights):
    states = [table(8, OWN), table(8, GHOST), table(8, GHOST)] * 2
    return sweep(
        dilatation_again, "dil1", pairs, counts, edges, tables, weights, states + N_TABLES,
        [LEFT, RIGHT, pltpu.VMEM((EXT + 1, 8, PTS), F32)],
    )


def run_force(pairs, counts, edges, tables, weights):
    return sweep(
        force_pass, "force", pairs, counts, edges, tables, weights, [table(1, OWN)] + F_TABLES,
        [
            LEFT,
            RIGHT,
            pltpu.VMEM((EXT, 16, 2 * PTS), BF16),
            pltpu.VMEM((EXT + 1, 16, PTS), F32),
            pltpu.VMEM((1, EXT * PTS), F32),
            pltpu.VMEM((EXT, 8, PTS), F32),
            pltpu.VMEM((CL, PTS, 8), F32),
        ],
    )


def run_pack(edges, *args):
    return pl.pallas_call(
        pack_kernel,
        out_shape=[table(8, OWN), table(8, OWN), table(8, PTS), table(16, GHOST), table(16, GHOST)],
        in_specs=[SMEM] + [VMEM] * 6,
        out_specs=[VMEM] * 5,
        name="pack",
    )(edges, *args)


def run_finish(edges, *args):
    return pl.pallas_call(
        finish_kernel,
        out_shape=[table(3, OWN), table(3, OWN)],
        in_specs=[SMEM] + [VMEM] * 7,
        out_specs=[VMEM] * 2,
        name="finish",
    )(edges, *args)


def lower(block, axis, ring):
    n = lax.axis_size(axis)
    route = [(i, (i - 1) % n) for i in range(n) if ring or i > 0]
    return lax.ppermute(block, axis, route)


def upper(block, axis, ring):
    n = lax.axis_size(axis)
    route = [(i, (i + 1) % n) for i in range(n) if ring or i < n - 1]
    return lax.ppermute(block, axis, route)


def exchange(part_c, part_a, own_c, own_a):
    return (
        lower(own_c, "circ", True),
        lower(own_a, "axial", False),
        upper(part_c, "circ", True),
        upper(part_a, "axial", False),
    )


def body(
    position, displacement, velocity, bulk, shear, volume, edges, block_pairs, block_counts, damage
):
    x = position.reshape(3, OWN)
    u = displacement.reshape(3, OWN)
    v = velocity.reshape(3, OWN)
    flat = lambda t: t.reshape(1, OWN)
    edge = edges[0, 0]
    pairs = block_pairs[0, 0]
    counts = block_counts[0, 0]
    s_own, v_own, mean, send_c, send_a = run_pack(
        edge, x, u, v, flat(bulk), flat(shear), flat(volume)
    )
    s_start = s_own
    got_c = lower(send_c, "circ", True)
    got_a = lower(send_a, "axial", False)
    s_c, s_a = got_c[:8], got_a[:8]
    v_c, v_a = got_c[8:], got_a[8:]
    weights, n_own, n_c, n_a, send_c, send_a = run_first(
        pairs, counts, edge, s_own, s_c, s_a, mean, damage[0, 0]
    )
    for step in range(STEPS):
        got = exchange(n_c, n_a, send_c, send_a)
        theta, f_own, f_c, f_a, send_c, send_a = run_force(
            pairs, counts, edge,
            [s_own, s_c, s_a, v_own, v_c, v_a, mean, n_own, n_c, n_a, *got],
            weights,
        )
        if step == STEPS - 1:
            back_c = upper(f_c, "circ", True)
            back_a = upper(f_a, "axial", False)
            u_out, vel_out = run_finish(edge, u, s_start, s_own, v_own, f_own, back_c, back_a)
        else:
            got = exchange(f_c, f_a, send_c, send_a)
            s_own, s_c, s_a, v_own, v_c, v_a, n_own, n_c, n_a, send_c, send_a = run_again(
                pairs, counts, edge,
                [s_own, s_c, s_a, v_own, v_c, v_a, mean, f_own, f_c, f_a, *got],
                weights,
            )
    wide = lambda t: t.reshape(t.shape[0], 1, 1, OWN)
    return wide(u_out), wide(vel_out), theta.reshape(1, 1, OWN)


def solution(mesh):
    placed = (
        P(None, "circ", "axial", None),
        P(None, "circ", "axial", None),
        P(None, "circ", "axial", None),
        P("circ", "axial", None),
        P("circ", "axial", None),
        P("circ", "axial", None),
        P("circ", "axial", None, None),
        P("circ", "axial", None, None),
        P("circ", "axial", None),
        P("circ", "axial", None, None, None),
    )
    return jax.shard_map(
        body,
        mesh=mesh,
        in_specs=placed,
        out_specs=(
            P(None, "circ", "axial", None),
            P(None, "circ", "axial", None),
            P("circ", "axial", None),
        ),
        check_vma=False,
    )
```

```python
import functools

import jax
import jax.numpy as jnp
from jax import lax
from jax.experimental import pallas as pl
from jax.experimental.pallas import tpu as pltpu
from jax.sharding import PartitionSpec as P

PTS = 128
CL = 128
FACING = 32
EXT = CL + 2 * FACING
SLOTS = 320
STEPS = 2
TIMESTEP = 0.07
SOFTEN = 0.01
LOG2E = 1.4426950408889634
KAPPA = LOG2E**0.5
TINY = 1e-30
GROUP = 32
UNROLL = 16
OWN = CL * PTS
GHOST = FACING * PTS
F32 = jnp.float32
BF16 = jnp.bfloat16
NT = (((1,), (1,)), ((), ()))
NN = (((1,), (0,)), ((), ()))


def dot(a, b, dims):
    return lax.dot_general(a, b, dims, preferred_element_type=F32)


def split3(x):
    h = x.astype(BF16).astype(F32)
    rest = x - h
    m = rest.astype(BF16).astype(F32)
    return h, m, rest - m


def hilo(x):
    h = x.astype(BF16)
    return h, (x - h.astype(F32)).astype(BF16)


def rows8():
    return lax.broadcasted_iota(jnp.int32, (8, PTS), 0)


def coordinate_parts(s):
    row = rows8()
    sq = s * s
    nx = sq[0:1] + sq[1:2] + sq[2:3]
    ny = sq[4:5] + sq[5:6] + sq[6:7]
    full = jnp.where(row == 3, nx, jnp.where(row == 7, ny, s))
    return split3(full)


def source_features(parts):
    p0, p1, p2 = parts
    one = jnp.ones((8, PTS), F32)
    stack = jnp.concatenate([p0, p0, p0, p1, p1, p2, one, one], axis=0)
    return jnp.transpose(stack).astype(BF16)


def target_features(parts):
    p0, p1, p2 = parts
    row = rows8()
    norm = (row == 3) | (row == 7)
    a0 = jnp.where(norm, -1.0, 2.0 * p0)
    a1 = jnp.where(norm, 0.0, 2.0 * p1)
    a2 = jnp.where(norm, 0.0, 2.0 * p2)
    n0 = jnp.where(norm, -p0, 0.0)
    shifted = pltpu.roll(p2, 1, 0)
    n1 = jnp.where(norm, -p1, 0.0)
    upper = row < 4
    after = (row == 4) | (row == 0)
    stack = jnp.concatenate([a0, a1, a2, a0, a1, a0], axis=0)
    up6 = jnp.concatenate([upper] * 6, axis=0)

    def half(top):
        keep = up6 if top else ~up6
        body = jnp.where(keep, stack, 0.0)
        near = upper if top else ~upper
        tail0 = jnp.where(near, n0, 0.0)
        tail1 = jnp.where(near, n1, 0.0) - jnp.where(row == (4 if top else 0), shifted, 0.0)
        return jnp.concatenate([body, tail0, tail1], axis=0).astype(BF16)

    return half(True), half(False)


def moment_features(parts):
    p0, p1, p2 = parts
    row = rows8()
    first = jnp.where(row == 3, 1.0, jnp.where(row > 3, p0, 0.0))
    first = jnp.where(row == 7, 0.0, first)
    second = jnp.where((row > 3) & (row < 7), p1, 0.0) + jnp.where(
        row < 3, pltpu.roll(p2, 4, 0), 0.0
    )
    m = jnp.concatenate([first, second], axis=0).astype(BF16)
    return jnp.concatenate([m, m], axis=1)


def coef_features(minus, neg_dev):
    row = rows8()
    pair = jnp.where(row == 0, minus, jnp.where(row == 1, neg_dev, 0.0))
    h, m, l = split3(pair)
    q = h + pltpu.roll(m, 2, 0) + pltpu.roll(l, 4, 0)
    even = (row == 0) | (row == 2) | (row == 4)
    odd = (row == 1) | (row == 3) | (row == 5)
    src = jnp.transpose(jnp.concatenate([q, jnp.ones((8, PTS), F32)], axis=0)).astype(BF16)
    t0 = jnp.concatenate([jnp.where(even, 1.0, 0.0), jnp.where(even, q, 0.0)], axis=0)
    t1 = jnp.concatenate([jnp.where(odd, 1.0, 0.0), jnp.where(odd, q, 0.0)], axis=0)
    return src, t0.astype(BF16), t1.astype(BF16)


def one_row(c):
    return pl.ds(c, 1)


def loop(n, fn, unroll):
    lax.fori_loop(0, n, lambda c, _: (fn(c), 0)[1], 0, unroll=unroll)


def pack_kernel(edges, x_ref, u_ref, v_ref, bulk, shear, volume, s_out, v_out, mean,
                sc_out, sa_out, vc_out, va_out):
    zero = jnp.zeros((1, PTS), F32)

    def cluster(c):
        r = one_row(c)
        x = [KAPPA * x_ref[k, r, :] for k in range(3)]
        y = [x[k] + KAPPA * u_ref[k, r, :] for k in range(3)]
        s_out[c] = jnp.concatenate([*x, zero, *y, zero], axis=0)
        inv = 1.0 / volume[r, :]
        mu = shear[r, :]
        dil = (3.0 * bulk[r, :] - 5.0 * mu) * inv
        dev = 15.0 * mu * inv
        thr = (3.0 / LOG2E) * inv
        v = [KAPPA * v_ref[k, r, :] for k in range(3)]
        v_out[c] = jnp.concatenate([dil, dev, thr, zero, *v, zero], axis=0)

    loop(CL, cluster, 4)
    total = jnp.sum(jnp.sum(s_out[...], axis=0), axis=1, keepdims=True)
    mean[...] = jnp.broadcast_to(total * (1.0 / OWN), (8, PTS))

    def copy(f):
        for side, s, v in ((0, sc_out, vc_out), (1, sa_out, va_out)):
            e = edges[side, f]
            s[f] = s_out[e]
            v[f] = v_out[e]

    loop(FACING, copy, 4)


def build_geometry(c, s, left, right, moments):
    parts = coordinate_parts(s)
    if left is not None:
        left[c] = source_features(parts)
    t0, t1 = target_features(parts)
    right[c, :, 0:PTS] = t0
    right[c, :, PTS:] = t1
    if moments is not None:
        moments[c] = moment_features(parts)


def build_all(s_own, s_c, s_a, mean, left, right, moments):
    shift = mean[...]
    loop(CL, lambda c: build_geometry(c, s_own[c] - shift, left, right, moments), 4)

    def ghost(f):
        build_geometry(CL + f, s_c[f] - shift, None, right, moments)
        build_geometry(CL + FACING + f, s_a[f] - shift, None, right, moments)

    loop(FACING, ghost, 2)


def turns_here(counts):
    g = pl.program_id(0)
    left_over = (counts[1] - g * GROUP + UNROLL - 1) // UNROLL
    return g, jnp.clip(left_over, 0, GROUP // UNROLL)


def first_sweep(pairs, counts, weight_of, left, right, acc, racc):
    g, turns = turns_here(counts)

    def turn(i, _):
        for j in range(UNROLL):
            k = i * UNROLL + j
            slot = g * GROUP + k
            p = pairs[0, slot]
            q = pairs[1, slot]
            live = slot < counts[1]
            ab = dot(left[p], right[q], NN)
            na = ab[:, :PTS]
            nb = ab[:, PTS:]
            w = weight_of(na, k, slot)
            x = jnp.maximum(na * nb, TINY)
            t = (x * lax.rsqrt(x) + na) * w
            acc[jnp.where(live, q, EXT)] += jnp.sum(t.reshape(16, 8, PTS), axis=0)
            racc[jnp.where(live, p, CL)] += t
        return 0

    lax.fori_loop(0, turns, turn, 0)


def first_finish(edges, acc, racc, n_own, n_c, n_a, send_c, send_a):
    ones = jnp.ones((16, 2 * PTS), BF16)

    def own(c):
        h, l = hilo(racc[c])
        across = dot(ones, jnp.concatenate([h, l], axis=1), NT)
        n_own[one_row(c), :] = across[0:1] + jnp.sum(acc[c], axis=0, keepdims=True)

    loop(CL, own, 4)

    def ghost(f):
        r = one_row(f)
        n_c[r, :] = jnp.sum(acc[CL + f], axis=0, keepdims=True)
        n_a[r, :] = jnp.sum(acc[CL + FACING + f], axis=0, keepdims=True)
        send_c[r, :] = n_own[one_row(edges[0, f]), :]
        send_a[r, :] = n_own[one_row(edges[1, f]), :]

    loop(FACING, ghost, 4)


def clear(ref):
    loop(ref.shape[0], lambda c: ref.__setitem__(c, jnp.zeros(ref.shape[1:], ref.dtype)), 1)


def dilatation_first(
    pairs, counts, edges, s_own, s_c, s_a, mean, damage,
    w_out, n_own, n_c, n_a, send_c, send_a,
    left, right, acc, racc, cut,
):
    g = pl.program_id(0)

    @pl.when(g == 0)
    def _():
        clear(acc)
        clear(racc)
        i0 = lax.broadcasted_iota(jnp.int32, (PTS, PTS), 0)
        i1 = lax.broadcasted_iota(jnp.int32, (PTS, PTS), 1)
        cut[0] = jnp.where(i0 < i1, 0, 1)
        cut[1] = jnp.zeros((PTS, PTS), jnp.int32)
        build_all(s_own, s_c, s_a, mean, left, right, None)

    def weight_of(na, k, slot):
        keep = damage[k] > cut[jnp.where(slot < CL, 0, 1)]
        w = jnp.where(keep, jnp.exp2(na), 0.0)
        w_out[k] = w
        return w

    first_sweep(pairs, counts, weight_of, left, right, acc, racc)

    @pl.when(g == pl.num_programs(0) - 1)
    def _():
        first_finish(edges, acc, racc, n_own, n_c, n_a, send_c, send_a)


def dilatation_again(
    pairs, counts, edges, s_own, s_c, s_a, v_own, v_c, v_a, mean, f_own, f_c, f_a,
    up_c, up_a, back_c, back_a, weights,
    s_own2, s_c2, s_a2, v_own2, v_c2, v_a2, n_own, n_c, n_a, send_c, send_a,
    left, right, acc, racc,
):
    g = pl.program_id(0)

    @pl.when(g == 0)
    def _():
        clear(acc)
        clear(racc)
        advance(edges, s_own, s_c, s_a, v_own, v_c, v_a, f_own, f_c, f_a, up_c, up_a, back_c,
                back_a, s_own2, s_c2, s_a2, v_own2, v_c2, v_a2)
        build_all(s_own2, s_c2, s_a2, mean, left, right, None)

    first_sweep(pairs, counts, lambda na, k, slot: weights[k], left, right, acc, racc)

    @pl.when(g == pl.num_programs(0) - 1)
    def _():
        first_finish(edges, acc, racc, n_own, n_c, n_a, send_c, send_a)


def advance(edges, s_own, s_c, s_a, v_own, v_c, v_a, f_own, f_c, f_a, up_c, up_a, back_c, back_a,
            s_own2, s_c2, s_a2, v_own2, v_c2, v_a2):
    pad = jnp.zeros((4, PTS), F32)

    def moved(s, v, f):
        v2 = v + TIMESTEP * jnp.concatenate([pad, f], axis=0)
        return s + jnp.where(rows8() < 4, 0.0, TIMESTEP * v2), v2

    def own(c):
        s_own2[c], v_own2[c] = moved(s_own[c], v_own[c], f_own[c])

    loop(CL, own, 8)

    def ghost(f):
        for side, back in ((0, back_c), (1, back_a)):
            e = edges[side, f]
            s_own2[e], v_own2[e] = moved(s_own[e], v_own[e], f_own[e] + back[f])
        s_c2[f], v_c2[f] = moved(s_c[f], v_c[f], up_c[f] + f_c[f])
        s_a2[f], v_a2[f] = moved(s_a[f], v_a[f], up_a[f] + f_a[f])

    loop(FACING, ghost, 4)


def force_pass(
    pairs, counts, edges, s_own, s_c, s_a, v_own, v_c, v_a, mean, n_own, n_c, n_a,
    up_c, up_a, back_c, back_a, weights,
    theta_out, f_own, f_c, f_a, send_c, send_a,
    left, right, left2, right2, moments, acc, n_full, geo, halves,
):
    def geometry(slot, j):
        s = jnp.minimum(slot, SLOTS - 1)
        p = pairs[0, s]
        q = pairs[1, s]
        geo[j, :, 0 : 2 * PTS] = dot(left[p], right[q], NN)
        geo[j, :, 2 * PTS :] = dot(left2[p], right2[q], NN)

    def chain(k, j):
        na = jnp.minimum(geo[j, :, 0:PTS], -TINY)
        nb = jnp.minimum(geo[j, :, PTS : 2 * PTS], -TINY)
        nu = nb - SOFTEN * LOG2E
        za = na * lax.rsqrt(na * nu)
        zb = nb * lax.rsqrt(nb * nu)
        m = weights[k] * (geo[j, :, 2 * PTS : 3 * PTS] * za + geo[j, :, 3 * PTS :] * zb)
        h, l = hilo(m)
        halves[j, 0:PTS, :] = h
        halves[j, PTS:, :] = l

    def gather(slot, j):
        s = jnp.maximum(slot, 0)
        p = pairs[0, s]
        q = pairs[1, s]
        live = (slot >= 0) & (slot < counts[1])
        hl = halves[j]
        gq = dot(moments[p], hl, NN)
        gp = dot(moments[q], jnp.concatenate([hl[:PTS], hl[PTS:]], axis=1), NT)
        return jnp.where(live, p, EXT), jnp.where(live, q, EXT), gp, gq

    def flush(found):
        for pa, qa, gp, gq in found:
            acc[qa] += gq
            acc[pa] += gp

    g, turns = turns_here(counts)

    @pl.when(g == 0)
    def _():
        clear(acc)
        build_all(s_own, s_c, s_a, mean, left, right, moments)
        n_full[0:CL, :] = n_own[...]

        def mend(f):
            r = one_row(f)
            for side, back in ((0, back_c), (1, back_a)):
                e = one_row(edges[side, f])
                n_full[e, :] = n_own[e, :] + back[r, :]
            n_full[one_row(CL + f), :] = up_c[r, :] + n_c[r, :]
            n_full[one_row(CL + FACING + f), :] = up_a[r, :] + n_a[r, :]

        loop(FACING, mend, 4)

        def coefs(c, v):
            theta = v[2:3] * n_full[one_row(c), :]
            src, t0, t1 = coef_features(v[1:2] - v[0:1] * theta, -v[1:2])
            right2[c, :, 0:PTS] = t0
            right2[c, :, PTS:] = t1
            return theta, src

        def own(c):
            theta, src = coefs(c, v_own[c])
            theta_out[one_row(c), :] = theta
            left2[c] = src

        loop(CL, own, 4)

        def ghost(f):
            coefs(CL + f, v_c[f])
            coefs(CL + FACING + f, v_a[f])

        loop(FACING, ghost, 4)
        for j in range(UNROLL):
            geometry(j, j)

    def turn(i, _):
        base = g * GROUP + i * UNROLL
        found = []
        for j in range(UNROLL + 1):
            if j < UNROLL:
                found.append(gather(base - UNROLL + j, j))
            if j > 0:
                chain(i * UNROLL + j - 1, j - 1)
                geometry(base + UNROLL + j - 1, j - 1)
        flush(found)
        return 0

    lax.fori_loop(0, turns, turn, 0)

    @pl.when(g == pl.num_programs(0) - 1)
    def _():
        last = (counts[1] + UNROLL - 1) // UNROLL * UNROLL - UNROLL
        flush([gather(last + j, j) for j in range(UNROLL)])
        shift = mean[...]

        def force(c, s):
            gsum = acc[c]
            first, second = gsum[0:8], gsum[8:16]
            total = first + second + pltpu.roll(second, 4, 0)
            return (total - (s - shift) * first[3:4])[4:8]

        def own(c):
            f_own[c] = force(c, s_own[c])

        loop(CL, own, 4)

        def ghost(f):
            f_c[f] = force(CL + f, s_c[f])
            f_a[f] = force(CL + FACING + f, s_a[f])
            send_c[f] = f_own[edges[0, f]]
            send_a[f] = f_own[edges[1, f]]

        loop(FACING, ghost, 4)


def finish_kernel(edges, u_ref, s_start, s_own, v_own, f_own, back_c, back_a, u_out, vel_out, f_sum):
    f_sum[...] = f_own[...]

    def mend(f):
        for side, back in ((0, back_c), (1, back_a)):
            e = edges[side, f]
            f_sum[e] = f_sum[e] + back[f]

    loop(FACING, mend, 4)

    def cluster(c):
        r = one_row(c)
        v2 = v_own[c][4:8] + TIMESTEP * f_sum[c]
        vel = v2 * (1.0 / KAPPA)
        gone = ((s_own[c] - s_start[c])[4:8] + TIMESTEP * v2) * (1.0 / KAPPA)
        for k in range(3):
            vel_out[k, r, :] = vel[k : k + 1]
            u_out[k, r, :] = u_ref[k, r, :] + gone[k : k + 1]

    loop(CL, cluster, 4)


SMEM = pl.BlockSpec(memory_space=pltpu.SMEM)
VMEM = pl.BlockSpec(memory_space=pltpu.VMEM)


def table(*shape):
    return jax.ShapeDtypeStruct(shape, F32)


def slab_spec():
    def index(g, pairs, counts):
        return (jnp.minimum(g, (counts[1] - 1) // GROUP), 0, 0)

    return pl.BlockSpec((GROUP, PTS, PTS), index)


def sweep(kernel, name, pairs, counts, edges, tables, slab, out_tables, scratch, slab_out=None):
    def whole(x, **kw):
        return pl.BlockSpec(x.shape, lambda g, a, b: (0,) * x.ndim, **kw)

    outs = [whole(x) for x in out_tables]
    out_shape = list(out_tables)
    if slab_out is not None:
        outs = [slab_spec()] + outs
        out_shape = [slab_out] + out_shape
    return pl.pallas_call(
        kernel,
        out_shape=out_shape,
        grid_spec=pltpu.PrefetchScalarGridSpec(
            num_scalar_prefetch=2,
            grid=(SLOTS // GROUP,),
            in_specs=[SMEM] + [whole(x, pipeline_mode=pl.Buffered(1)) for x in tables] + [slab_spec()],
            out_specs=outs,
            scratch_shapes=scratch,
        ),
        compiler_params=pltpu.CompilerParams(
            dimension_semantics=("arbitrary",), vmem_limit_bytes=56 << 20
        ),
        name=name,
    )(pairs, counts, edges, *tables, slab)


LEFT = pltpu.VMEM((CL, PTS, 64), BF16)
RIGHT = pltpu.VMEM((EXT, 64, 2 * PTS), BF16)
N_TABLES = [table(CL, PTS)] + [table(FACING, PTS)] * 4
F_TABLES = [table(CL, 4, PTS)] + [table(FACING, 4, PTS)] * 4
STATES = [table(CL, 8, PTS), table(FACING, 8, PTS), table(FACING, 8, PTS)]
SUMS = [pltpu.VMEM((EXT + 1, 8, PTS), F32), pltpu.VMEM((CL + 1, PTS, PTS), F32)]


def run_first(pairs, counts, edges, s_own, s_c, s_a, mean, damage):
    return sweep(
        dilatation_first, "dil0", pairs, counts, edges, [s_own, s_c, s_a, mean], damage, N_TABLES,
        [LEFT, RIGHT, *SUMS, pltpu.VMEM((2, PTS, PTS), jnp.int32)],
        slab_out=table(SLOTS, PTS, PTS),
    )


def run_again(pairs, counts, edges, tables, weights):
    return sweep(
        dilatation_again, "dil1", pairs, counts, edges, tables, weights, STATES * 2 + N_TABLES,
        [LEFT, RIGHT, *SUMS],
    )


def run_force(pairs, counts, edges, tables, weights):
    return sweep(
        force_pass, "force", pairs, counts, edges, tables, weights, [table(CL, PTS)] + F_TABLES,
        [
            LEFT,
            RIGHT,
            pltpu.VMEM((CL, PTS, 16), BF16),
            pltpu.VMEM((EXT, 16, 2 * PTS), BF16),
            pltpu.VMEM((EXT, 16, 2 * PTS), BF16),
            pltpu.VMEM((EXT + 1, 16, PTS), F32),
            pltpu.VMEM((EXT, PTS), F32),
            pltpu.VMEM((UNROLL, PTS, 4 * PTS), F32),
            pltpu.VMEM((UNROLL, 2 * PTS, PTS), BF16),
        ],
    )


def run_pack(edges, *args):
    return pl.pallas_call(
        pack_kernel,
        out_shape=[table(CL, 8, PTS)] * 2 + [table(8, PTS)] + [table(FACING, 8, PTS)] * 4,
        in_specs=[SMEM] + [VMEM] * 6,
        out_specs=[VMEM] * 7,
        name="pack",
    )(edges, *args)


def run_finish(edges, *args):
    return pl.pallas_call(
        finish_kernel,
        out_shape=[table(3, CL, PTS), table(3, CL, PTS)],
        in_specs=[SMEM] + [VMEM] * 7,
        out_specs=[VMEM] * 2,
        scratch_shapes=[pltpu.VMEM((CL, 4, PTS), F32)],
        name="finish",
    )(edges, *args)


def shift_ring(block, axis, by):
    n = lax.axis_size(axis)
    return lax.ppermute(block, axis, [(i, (i + by) % n) for i in range(n)])


def exchange(part_c, part_a, own_c, own_a):
    return (
        shift_ring(own_c, "circ", -1),
        shift_ring(own_a, "axial", -1),
        shift_ring(part_c, "circ", 1),
        shift_ring(part_a, "axial", 1),
    )


def body(
    position, displacement, velocity, bulk, shear, volume, edges, block_pairs, block_counts, damage
):
    cube = lambda t: t.reshape(3, CL, PTS)
    flat = lambda t: t.reshape(CL, PTS)
    u = cube(displacement)
    edge = edges[0, 0]
    pairs = block_pairs[0, 0]
    counts = block_counts[0, 0]
    s_own, v_own, mean, s_c, s_a, v_c, v_a = run_pack(
        edge, cube(position), u, cube(velocity), flat(bulk), flat(shear), flat(volume)
    )
    s_start = s_own
    s_c = shift_ring(s_c, "circ", -1)
    s_a = shift_ring(s_a, "axial", -1)
    s_c, s_a, v_c, v_a = lax.optimization_barrier((s_c, s_a, v_c, v_a))
    v_c = shift_ring(v_c, "circ", -1)
    v_a = shift_ring(v_a, "axial", -1)
    weights, n_own, n_c, n_a, send_c, send_a = run_first(
        pairs, counts, edge, s_own, s_c, s_a, mean, damage[0, 0]
    )
    for step in range(STEPS):
        got = exchange(n_c, n_a, send_c, send_a)
        theta, f_own, f_c, f_a, send_c, send_a = run_force(
            pairs, counts, edge,
            [s_own, s_c, s_a, v_own, v_c, v_a, mean, n_own, n_c, n_a, *got],
            weights,
        )
        if step == STEPS - 1:
            back_c = shift_ring(f_c, "circ", 1)
            back_a = shift_ring(f_a, "axial", 1)
            u_out, vel_out = run_finish(edge, u, s_start, s_own, v_own, f_own, back_c, back_a)
        else:
            got = exchange(f_c, f_a, send_c, send_a)
            s_own, s_c, s_a, v_own, v_c, v_a, n_own, n_c, n_a, send_c, send_a = run_again(
                pairs, counts, edge,
                [s_own, s_c, s_a, v_own, v_c, v_a, mean, f_own, f_c, f_a, *got],
                weights,
            )
    wide = lambda t: t.reshape(3, 1, 1, OWN)
    return wide(u_out), wide(vel_out), theta.reshape(1, 1, OWN)


def solution(mesh):
    placed = (
        P(None, "circ", "axial", None),
        P(None, "circ", "axial", None),
        P(None, "circ", "axial", None),
        P("circ", "axial", None),
        P("circ", "axial", None),
        P("circ", "axial", None),
        P("circ", "axial", None, None),
        P("circ", "axial", None, None),
        P("circ", "axial", None),
        P("circ", "axial", None, None, None),
    )
    return jax.shard_map(
        body,
        mesh=mesh,
        in_specs=placed,
        out_specs=(
            P(None, "circ", "axial", None),
            P(None, "circ", "axial", None),
            P("circ", "axial", None),
        ),
        check_vma=False,
    )
```

```python
import functools

import jax
import jax.numpy as jnp
from jax import lax
from jax.experimental import pallas as pl
from jax.experimental.pallas import tpu as pltpu
from jax.sharding import PartitionSpec as P

PTS = 128
CL = 128
FACING = 32
EXT = CL + 2 * FACING
SLOTS = 320
STEPS = 2
TIMESTEP = 0.07
SOFTEN = 0.01
LOG2E = 1.4426950408889634
KAPPA = LOG2E**0.5
TINY = 1e-30
GROUP = 32
UNROLL = 16
KERNEL_VMEM = 36 << 20
OWN = CL * PTS
GHOST = FACING * PTS
F32 = jnp.float32
BF16 = jnp.bfloat16
NT = (((1,), (1,)), ((), ()))
NN = (((1,), (0,)), ((), ()))


def dot(a, b, dims):
    return lax.dot_general(a, b, dims, preferred_element_type=F32)


def split3(x):
    h = x.astype(BF16).astype(F32)
    rest = x - h
    m = rest.astype(BF16).astype(F32)
    return h, m, rest - m


def hilo(x):
    h = x.astype(BF16)
    return h, (x - h.astype(F32)).astype(BF16)


def rows8():
    return lax.broadcasted_iota(jnp.int32, (8, PTS), 0)


def coordinate_parts(s):
    row = rows8()
    sq = s * s
    nx = sq[0:1] + sq[1:2] + sq[2:3]
    ny = sq[4:5] + sq[5:6] + sq[6:7]
    full = jnp.where(row == 3, nx, jnp.where(row == 7, ny, s))
    return split3(full)


def source_features(parts):
    p0, p1, p2 = parts
    one = jnp.ones((8, PTS), F32)
    stack = jnp.concatenate([p0, p0, p0, p1, p1, p2, one, one], axis=0)
    return jnp.transpose(stack).astype(BF16)


def target_features(parts):
    p0, p1, p2 = parts
    row = rows8()
    norm = (row == 3) | (row == 7)
    a0 = jnp.where(norm, -1.0, 2.0 * p0)
    a1 = jnp.where(norm, 0.0, 2.0 * p1)
    a2 = jnp.where(norm, 0.0, 2.0 * p2)
    n0 = jnp.where(norm, -p0, 0.0)
    n1 = jnp.where(norm, -p1, 0.0)
    n2 = jnp.where((row == 2) | (row == 6), -pltpu.roll(p2, 7, 0), 0.0)
    stack = jnp.concatenate([a0, a1, a2, a0, a1, a0, n0, n1 + n2], axis=0).astype(BF16)
    top = (lax.broadcasted_iota(jnp.int32, (64, PTS), 0) & 4) == 0
    ones = jnp.where(top, 1.0, 0.0).astype(BF16)
    zeros = jnp.where(top, 0.0, 1.0).astype(BF16)
    return stack * ones, stack * zeros


def moment_features(parts):
    p0, p1, p2 = parts
    row = rows8()
    first = jnp.where(row == 3, 1.0, jnp.where(row > 3, p0, 0.0))
    first = jnp.where(row == 7, 0.0, first)
    second = jnp.where((row > 3) & (row < 7), p1, 0.0) + jnp.where(
        row < 3, pltpu.roll(p2, 4, 0), 0.0
    )
    m = jnp.concatenate([first, second], axis=0).astype(BF16)
    return jnp.concatenate([m, m], axis=1)


def coef_features(minus, neg_dev):
    row = rows8()
    pair = jnp.where(row == 0, minus, jnp.where(row == 1, neg_dev, 0.0))
    h, m, l = split3(pair)
    q = h + pltpu.roll(m, 2, 0) + pltpu.roll(l, 4, 0)
    even = (row == 0) | (row == 2) | (row == 4)
    odd = (row == 1) | (row == 3) | (row == 5)
    src = jnp.transpose(jnp.concatenate([q, jnp.ones((8, PTS), F32)], axis=0)).astype(BF16)
    t0 = jnp.concatenate([jnp.where(even, 1.0, 0.0), jnp.where(even, q, 0.0)], axis=0)
    t1 = jnp.concatenate([jnp.where(odd, 1.0, 0.0), jnp.where(odd, q, 0.0)], axis=0)
    return src, t0.astype(BF16), t1.astype(BF16)


def one_row(c):
    return pl.ds(c, 1)


def loop(n, fn, unroll):
    lax.fori_loop(0, n, lambda c, _: (fn(c), 0)[1], 0, unroll=unroll)


def pack_kernel(edges, x_ref, u_ref, v_ref, bulk, shear, volume, s_out, v_out, mean,
                sc_out, sa_out, vc_out, va_out):
    zero = jnp.zeros((8, PTS), F32)
    s_rows = s_out.reshape(CL * 8, PTS)
    v_rows = v_out.reshape(CL * 8, PTS)

    def eight(i):
        r = pl.ds(pl.multiple_of(i * 8, 8), 8)

        def put(ref, k, value):
            ref[pl.ds(i * 64 + k, 8, stride=8), :] = value

        x = [KAPPA * x_ref[k, r, :] for k in range(3)]
        y = [x[k] + KAPPA * u_ref[k, r, :] for k in range(3)]
        vol = volume[r, :]
        mu = shear[r, :]
        dil = (3.0 * bulk[r, :] - 5.0 * mu) / vol
        dev = 15.0 * mu / vol
        thr = (3.0 / LOG2E) / vol
        v = [KAPPA * v_ref[k, r, :] for k in range(3)]
        for k, value in enumerate([*x, zero, *y, zero]):
            put(s_rows, k, value)
        for k, value in enumerate([dil, dev, thr, zero, *v, zero]):
            put(v_rows, k, value)

    loop(CL // 8, eight, 2)
    total = jnp.sum(jnp.sum(s_out[...], axis=0), axis=1, keepdims=True)
    mean[...] = jnp.broadcast_to(total * (1.0 / OWN), (8, PTS))

    def copy(f):
        for side, s, v in ((0, sc_out, vc_out), (1, sa_out, va_out)):
            e = edges[side, f]
            s[f] = s_out[e]
            v[f] = v_out[e]

    loop(FACING, copy, 4)


def build_one(c, s, left, right, moments):
    parts = coordinate_parts(s)
    if left is not None:
        left[c] = source_features(parts)
    t0, t1 = target_features(parts)
    right[c, :, 0:PTS] = t0
    right[c, :, PTS:] = t1
    moments[c] = moment_features(parts)


def build_own(s_own, mean, left, right, moments):
    shift = mean[...]
    loop(CL, lambda c: build_one(c, s_own[c] - shift, left, right, moments), 4)


def build_ghosts(s_c, s_a, mean, right, moments):
    shift = mean[...]

    def ghost(f):
        build_one(CL + f, s_c[f] - shift, None, right, moments)
        build_one(CL + FACING + f, s_a[f] - shift, None, right, moments)

    loop(FACING, ghost, 4)


def ghosts_kernel(s_c, s_a, mean, right_in, moments_in, right, moments):
    build_ghosts(s_c, s_a, mean, right, moments)


def turns_here(counts):
    g = pl.program_id(0)
    left_over = (counts[1] - g * GROUP + UNROLL - 1) // UNROLL
    return g, jnp.clip(left_over, 0, GROUP // UNROLL)


def first_sweep(pairs, counts, weight_of, left, right, acc, racc):
    g, turns = turns_here(counts)

    def turn(i, _):
        for j in range(UNROLL):
            k = i * UNROLL + j
            slot = g * GROUP + k
            p = pairs[0, slot]
            q = pairs[1, slot]
            live = slot < counts[1]
            ab = dot(left[p], right[q], NN)
            na = ab[:, :PTS]
            nb = ab[:, PTS:]
            w = weight_of(na, k, slot)
            x = jnp.maximum(na * nb, TINY)
            t = (x * lax.rsqrt(x) + na) * w
            acc[jnp.where(live, q, EXT)] += jnp.sum(t.reshape(16, 8, PTS), axis=0)
            racc[jnp.where(live, p, CL)] += t
        return 0

    lax.fori_loop(0, turns, turn, 0)


def first_finish(edges, acc, racc, n_own, n_c, n_a, send_c, send_a):
    ones = jnp.ones((2 * PTS, PTS), BF16)
    i0 = lax.broadcasted_iota(jnp.int32, (PTS, PTS), 0)
    i1 = lax.broadcasted_iota(jnp.int32, (PTS, PTS), 1)
    diagonal = i0 == i1

    def own(c):
        h, l = hilo(racc[c])
        across = dot(jnp.concatenate([h, l], axis=1), ones, NN)
        along = jnp.sum(jnp.where(diagonal, across, 0.0).reshape(16, 8, PTS), axis=0)
        n_own[one_row(c), :] = jnp.sum(along + acc[c], axis=0, keepdims=True)

    loop(CL, own, 8)

    def ghost(f):
        r = one_row(f)
        n_c[r, :] = jnp.sum(acc[CL + f], axis=0, keepdims=True)
        n_a[r, :] = jnp.sum(acc[CL + FACING + f], axis=0, keepdims=True)
        send_c[r, :] = n_own[one_row(edges[0, f]), :]
        send_a[r, :] = n_own[one_row(edges[1, f]), :]

    loop(FACING, ghost, 4)


def clear(ref):
    n = ref.shape[0] // 8 * 8
    zero = jnp.zeros(ref.shape[1:], ref.dtype)

    def one(c):
        ref[c] = zero

    loop(n, one, 8)
    for c in range(n, ref.shape[0]):
        one(c)


def dilatation_first(
    pairs, counts, edges, left, right, damage,
    w_out, n_own, n_c, n_a, send_c, send_a,
    acc, racc, cut,
):
    g = pl.program_id(0)

    @pl.when(g == 0)
    def _():
        clear(acc)
        clear(racc)
        i0 = lax.broadcasted_iota(jnp.int32, (PTS, PTS), 0)
        i1 = lax.broadcasted_iota(jnp.int32, (PTS, PTS), 1)
        cut[0] = jnp.where(i0 < i1, 0, 1)
        cut[1] = jnp.zeros((PTS, PTS), jnp.int32)

    def weight_of(na, k, slot):
        keep = damage[k] > cut[jnp.where(slot < CL, 0, 1)]
        w = jnp.where(keep, jnp.exp2(na), 0.0)
        w_out[k] = w
        return w

    first_sweep(pairs, counts, weight_of, left, right, acc, racc)

    @pl.when(g == pl.num_programs(0) - 1)
    def _():
        first_finish(edges, acc, racc, n_own, n_c, n_a, send_c, send_a)


def advance_kernel(
    edges, s_own, s_c, s_a, v_own, v_c, v_a, mean, f_own, f_c, f_a, up_c, up_a, back_c, back_a,
    s_own2, s_c2, s_a2, v_own2, v_c2, v_a2, left, right, moments,
):
    advance(edges, s_own, s_c, s_a, v_own, v_c, v_a, f_own, f_c, f_a, up_c, up_a, back_c,
            back_a, s_own2, s_c2, s_a2, v_own2, v_c2, v_a2)
    build_own(s_own2, mean, left, right, moments)
    build_ghosts(s_c2, s_a2, mean, right, moments)


def dilatation_again(
    pairs, counts, edges, left, right, weights, n_own, n_c, n_a, send_c, send_a, acc, racc
):
    g = pl.program_id(0)

    @pl.when(g == 0)
    def _():
        clear(acc)
        clear(racc)

    first_sweep(pairs, counts, lambda na, k, slot: weights[k], left, right, acc, racc)

    @pl.when(g == pl.num_programs(0) - 1)
    def _():
        first_finish(edges, acc, racc, n_own, n_c, n_a, send_c, send_a)


def advance(edges, s_own, s_c, s_a, v_own, v_c, v_a, f_own, f_c, f_a, up_c, up_a, back_c, back_a,
            s_own2, s_c2, s_a2, v_own2, v_c2, v_a2):
    pad = jnp.zeros((4, PTS), F32)

    def moved(s, v, f):
        v2 = v + TIMESTEP * jnp.concatenate([pad, f], axis=0)
        return s + jnp.where(rows8() < 4, 0.0, TIMESTEP * v2), v2

    def own(c):
        s_own2[c], v_own2[c] = moved(s_own[c], v_own[c], f_own[c])

    loop(CL, own, 8)

    def ghost(f):
        for side, back in ((0, back_c), (1, back_a)):
            e = edges[side, f]
            s_own2[e], v_own2[e] = moved(s_own[e], v_own[e], f_own[e] + back[f])
        s_c2[f], v_c2[f] = moved(s_c[f], v_c[f], up_c[f] + f_c[f])
        s_a2[f], v_a2[f] = moved(s_a[f], v_a[f], up_a[f] + f_a[f])

    loop(FACING, ghost, 4)


def force_pass(
    pairs, counts, edges, left, right, moments, s_own, s_c, s_a, v_own, v_c, v_a, mean,
    n_own, n_c, n_a, up_c, up_a, back_c, back_a, weights,
    theta_out, f_own, f_c, f_a, send_c, send_a,
    left2, right2, acc, n_full, geo, halves,
):
    def geometry(slot, j):
        s = jnp.minimum(slot, SLOTS - 1)
        p = pairs[0, s]
        q = pairs[1, s]
        geo[j, :, 0 : 2 * PTS] = dot(left[p], right[q], NN)
        geo[j, :, 2 * PTS :] = dot(left2[p], right2[q], NN)

    def chain(k, j):
        na = jnp.minimum(geo[j, :, 0:PTS], -TINY)
        nb = jnp.minimum(geo[j, :, PTS : 2 * PTS], -TINY)
        nu = nb - SOFTEN * LOG2E
        za = na * lax.rsqrt(na * nu)
        zb = nb * lax.rsqrt(nb * nu)
        m = weights[k] * (geo[j, :, 2 * PTS : 3 * PTS] * za + geo[j, :, 3 * PTS :] * zb)
        h, l = hilo(m)
        halves[j, 0:PTS, :] = h
        halves[j, PTS:, :] = l

    def gather(slot, j):
        s = jnp.maximum(slot, 0)
        p = pairs[0, s]
        q = pairs[1, s]
        live = (slot >= 0) & (slot < counts[1])
        hl = halves[j]
        gq = dot(moments[p], hl, NN)
        gp = dot(moments[q], jnp.concatenate([hl[:PTS], hl[PTS:]], axis=1), NT)
        return jnp.where(live, p, EXT), jnp.where(live, q, EXT), gp, gq

    def flush(found):
        for pa, qa, gp, gq in found:
            acc[qa] += gq
            acc[pa] += gp

    g, turns = turns_here(counts)

    @pl.when(g == 0)
    def _():
        clear(acc)
        n_full[0:CL, :] = n_own[...]

        def mend(f):
            r = one_row(f)
            for side, back in ((0, back_c), (1, back_a)):
                e = one_row(edges[side, f])
                n_full[e, :] = n_own[e, :] + back[r, :]
            n_full[one_row(CL + f), :] = up_c[r, :] + n_c[r, :]
            n_full[one_row(CL + FACING + f), :] = up_a[r, :] + n_a[r, :]

        loop(FACING, mend, 4)

        def coefs(c, v):
            theta = v[2:3] * n_full[one_row(c), :]
            src, t0, t1 = coef_features(v[1:2] - v[0:1] * theta, -v[1:2])
            right2[c, :, 0:PTS] = t0
            right2[c, :, PTS:] = t1
            return theta, src

        def own(c):
            theta, src = coefs(c, v_own[c])
            theta_out[one_row(c), :] = theta
            left2[c] = src

        loop(CL, own, 4)

        def ghost(f):
            coefs(CL + f, v_c[f])
            coefs(CL + FACING + f, v_a[f])

        loop(FACING, ghost, 4)
        for j in range(UNROLL):
            geometry(j, j)

    def turn(i, _):
        base = g * GROUP + i * UNROLL
        found = []
        for j in range(UNROLL + 1):
            if j < UNROLL:
                found.append(gather(base - UNROLL + j, j))
            if j > 0:
                chain(i * UNROLL + j - 1, j - 1)
                geometry(base + UNROLL + j - 1, j - 1)
        flush(found)
        return 0

    lax.fori_loop(0, turns, turn, 0)

    @pl.when(g == pl.num_programs(0) - 1)
    def _():
        last = (counts[1] + UNROLL - 1) // UNROLL * UNROLL - UNROLL
        flush([gather(last + j, j) for j in range(UNROLL)])
        shift = mean[...]

        def force(c, s):
            gsum = acc[c]
            first, second = gsum[0:8], gsum[8:16]
            total = first + second + pltpu.roll(second, 4, 0)
            return (total - (s - shift) * first[3:4])[4:8]

        def own(c):
            f_own[c] = force(c, s_own[c])

        loop(CL, own, 4)

        def ghost(f):
            f_c[f] = force(CL + f, s_c[f])
            f_a[f] = force(CL + FACING + f, s_a[f])
            send_c[f] = f_own[edges[0, f]]
            send_a[f] = f_own[edges[1, f]]

        loop(FACING, ghost, 4)


def finish_kernel(edges, u_ref, s_start, s_own, v_own, f_own, back_c, back_a, u_out, vel_out, f_sum):
    f_sum[...] = f_own[...]

    def mend(f):
        for side, back in ((0, back_c), (1, back_a)):
            e = edges[side, f]
            f_sum[e] = f_sum[e] + back[f]

    loop(FACING, mend, 4)

    views = [t.reshape(CL * 8, PTS) for t in (s_own, s_start, v_own)]
    f_rows = f_sum.reshape(CL * 4, PTS)

    def eight(i):
        r = pl.ds(pl.multiple_of(i * 8, 8), 8)
        for k in range(3):
            now, start, vel = (t[pl.ds(i * 64 + 4 + k, 8, stride=8), :] for t in views)
            vel = vel + TIMESTEP * f_rows[pl.ds(i * 32 + k, 8, stride=4), :]
            vel_out[k, r, :] = vel * (1.0 / KAPPA)
            gone = (now - start) + TIMESTEP * vel
            u_out[k, r, :] = u_ref[k, r, :] + gone * (1.0 / KAPPA)

    loop(CL // 8, eight, 2)


SMEM = pl.BlockSpec(memory_space=pltpu.SMEM)
VMEM = pl.BlockSpec(memory_space=pltpu.VMEM)


def table(*shape):
    return jax.ShapeDtypeStruct(shape, F32)


def slab_spec():
    def index(g, pairs, counts):
        return (jnp.minimum(g, (counts[1] - 1) // GROUP), 0, 0)

    return pl.BlockSpec((GROUP, PTS, PTS), index)


def sweep(
    kernel, name, pairs, counts, edges, resident, tables, slab, out_tables, scratch, slab_out=None
):
    def whole(x, **kw):
        return pl.BlockSpec(x.shape, lambda g, a, b: (0,) * x.ndim, **kw)

    outs = [whole(x) for x in out_tables]
    out_shape = list(out_tables)
    if slab_out is not None:
        outs = [slab_spec()] + outs
        out_shape = [slab_out] + out_shape
    return pl.pallas_call(
        kernel,
        out_shape=out_shape,
        grid_spec=pltpu.PrefetchScalarGridSpec(
            num_scalar_prefetch=2,
            grid=(SLOTS // GROUP,),
            in_specs=[SMEM]
            + [VMEM] * len(resident)
            + [whole(x, pipeline_mode=pl.Buffered(1)) for x in tables]
            + [slab_spec()],
            out_specs=outs,
            scratch_shapes=scratch,
        ),
        compiler_params=pltpu.CompilerParams(
            dimension_semantics=("arbitrary",), vmem_limit_bytes=KERNEL_VMEM
        ),
        name=name,
    )(pairs, counts, edges, *resident, *tables, slab)


LEFT = jax.ShapeDtypeStruct((CL, PTS, 64), BF16)
RIGHT = jax.ShapeDtypeStruct((EXT, 64, 2 * PTS), BF16)
MOMENTS = jax.ShapeDtypeStruct((EXT, 16, 2 * PTS), BF16)
N_TABLES = [table(CL, PTS)] + [table(FACING, PTS)] * 4
F_TABLES = [table(CL, 4, PTS)] + [table(FACING, 4, PTS)] * 4
STATES = [table(CL, 8, PTS), table(FACING, 8, PTS), table(FACING, 8, PTS)]
SUMS = [pltpu.VMEM((EXT + 1, 8, PTS), F32), pltpu.VMEM((CL + 1, PTS, PTS), F32)]


def small(kernel, name, out_shape, args, smem=0, aliases=None):
    return pl.pallas_call(
        kernel,
        out_shape=out_shape,
        in_specs=[SMEM] * smem + [VMEM] * (len(args) - smem),
        out_specs=[VMEM] * len(out_shape),
        input_output_aliases=aliases or {},
        compiler_params=pltpu.CompilerParams(vmem_limit_bytes=KERNEL_VMEM),
        name=name,
    )(*args)


def run_build(s_own, mean):
    return small(build_own, "build", [LEFT, RIGHT, MOMENTS], [s_own, mean])


def run_ghosts(s_c, s_a, mean, right, moments):
    return small(
        ghosts_kernel, "ghosts", [RIGHT, MOMENTS], [s_c, s_a, mean, right, moments],
        aliases={3: 0, 4: 1},
    )


def run_advance(edges, tables):
    return small(
        advance_kernel, "advance", STATES * 2 + [LEFT, RIGHT, MOMENTS], [edges, *tables], smem=1
    )


def run_first(pairs, counts, edges, resident, damage):
    return sweep(
        dilatation_first, "dil0", pairs, counts, edges, resident, [], damage, N_TABLES,
        [*SUMS, pltpu.VMEM((2, PTS, PTS), jnp.int32)],
        slab_out=table(SLOTS, PTS, PTS),
    )


def run_again(pairs, counts, edges, resident, weights):
    return sweep(
        dilatation_again, "dil1", pairs, counts, edges, resident, [], weights, N_TABLES, SUMS
    )


def run_force(pairs, counts, edges, resident, tables, weights):
    return sweep(
        force_pass, "force", pairs, counts, edges, resident, tables, weights,
        [table(CL, PTS)] + F_TABLES,
        [
            pltpu.VMEM((CL, PTS, 16), BF16),
            pltpu.VMEM((EXT, 16, 2 * PTS), BF16),
            pltpu.VMEM((EXT + 1, 16, PTS), F32),
            pltpu.VMEM((EXT, PTS), F32),
            pltpu.VMEM((UNROLL, PTS, 4 * PTS), F32),
            pltpu.VMEM((UNROLL, 2 * PTS, PTS), BF16),
        ],
    )


def run_pack(edges, *args):
    return pl.pallas_call(
        pack_kernel,
        out_shape=[table(CL, 8, PTS)] * 2 + [table(8, PTS)] + [table(FACING, 8, PTS)] * 4,
        in_specs=[SMEM] + [VMEM] * 6,
        out_specs=[VMEM] * 7,
        name="pack",
    )(edges, *args)


def run_finish(edges, *args):
    return pl.pallas_call(
        finish_kernel,
        out_shape=[table(3, CL, PTS), table(3, CL, PTS)],
        in_specs=[SMEM] + [VMEM] * 7,
        out_specs=[VMEM] * 2,
        scratch_shapes=[pltpu.VMEM((CL, 4, PTS), F32)],
        name="finish",
    )(edges, *args)


def shift_ring(block, axis, by):
    n = lax.axis_size(axis)
    return lax.ppermute(block, axis, [(i, (i + by) % n) for i in range(n)])


def exchange(part_c, part_a, own_c, own_a):
    return (
        shift_ring(own_c, "circ", -1),
        shift_ring(own_a, "axial", -1),
        shift_ring(part_c, "circ", 1),
        shift_ring(part_a, "axial", 1),
    )


def body(
    position, displacement, velocity, bulk, shear, volume, edges, block_pairs, block_counts, damage
):
    cube = lambda t: t.reshape(3, CL, PTS)
    flat = lambda t: t.reshape(CL, PTS)
    u = cube(displacement)
    edge = edges[0, 0]
    pairs = block_pairs[0, 0]
    counts = block_counts[0, 0]
    s_own, v_own, mean, s_c, s_a, v_c, v_a = run_pack(
        edge, cube(position), u, cube(velocity), flat(bulk), flat(shear), flat(volume)
    )
    s_start = s_own
    s_c = shift_ring(s_c, "circ", -1)
    s_a = shift_ring(s_a, "axial", -1)
    left, right, moments = run_build(s_own, mean)
    s_c, s_a, v_c, v_a = lax.optimization_barrier((s_c, s_a, v_c, v_a))
    right, moments = run_ghosts(s_c, s_a, mean, right, moments)
    v_c = shift_ring(v_c, "circ", -1)
    v_a = shift_ring(v_a, "axial", -1)
    weights, n_own, n_c, n_a, send_c, send_a = run_first(
        pairs, counts, edge, [left, right], damage[0, 0]
    )
    for step in range(STEPS):
        got = exchange(n_c, n_a, send_c, send_a)
        theta, f_own, f_c, f_a, send_c, send_a = run_force(
            pairs, counts, edge, [left, right, moments],
            [s_own, s_c, s_a, v_own, v_c, v_a, mean, n_own, n_c, n_a, *got],
            weights,
        )
        if step == STEPS - 1:
            back_c = shift_ring(f_c, "circ", 1)
            back_a = shift_ring(f_a, "axial", 1)
            u_out, vel_out = run_finish(edge, u, s_start, s_own, v_own, f_own, back_c, back_a)
        else:
            got = exchange(f_c, f_a, send_c, send_a)
            s_own, s_c, s_a, v_own, v_c, v_a, left, right, moments = run_advance(
                edge, [s_own, s_c, s_a, v_own, v_c, v_a, mean, f_own, f_c, f_a, *got]
            )
            n_own, n_c, n_a, send_c, send_a = run_again(
                pairs, counts, edge, [left, right], weights
            )
    wide = lambda t: t.reshape(3, 1, 1, OWN)
    return wide(u_out), wide(vel_out), theta.reshape(1, 1, OWN)


def solution(mesh):
    placed = (
        P(None, "circ", "axial", None),
        P(None, "circ", "axial", None),
        P(None, "circ", "axial", None),
        P("circ", "axial", None),
        P("circ", "axial", None),
        P("circ", "axial", None),
        P("circ", "axial", None, None),
        P("circ", "axial", None, None),
        P("circ", "axial", None),
        P("circ", "axial", None, None, None),
    )
    return jax.shard_map(
        body,
        mesh=mesh,
        in_specs=placed,
        out_specs=(
            P(None, "circ", "axial", None),
            P(None, "circ", "axial", None),
            P("circ", "axial", None),
        ),
        check_vma=False,
    )
```

```python
import functools

import jax
import jax.numpy as jnp
from jax import lax
from jax.experimental import pallas as pl
from jax.experimental.pallas import tpu as pltpu
from jax.sharding import PartitionSpec as P

PTS = 128
CL = 128
FACING = 32
EXT = CL + 2 * FACING
SLOTS = 320
STEPS = 2
TIMESTEP = 0.07
SOFTEN = 0.01
LOG2E = 1.4426950408889634
KAPPA = LOG2E**0.5
TINY = 1e-30
GROUP = 32
UNROLL = 16
FORCE_UNROLL = 16
KERNEL_VMEM = 21 << 20
OWN = CL * PTS
GHOST = FACING * PTS
F32 = jnp.float32
BF16 = jnp.bfloat16
NT = (((1,), (1,)), ((), ()))
NN = (((1,), (0,)), ((), ()))


def dot(a, b, dims):
    return lax.dot_general(a, b, dims, preferred_element_type=F32)


def split3(x):
    h = x.astype(BF16).astype(F32)
    rest = x - h
    m = rest.astype(BF16).astype(F32)
    return h, m, rest - m


def hilo(x):
    h = x.astype(BF16)
    return h, (x - h.astype(F32)).astype(BF16)


def rows8():
    return lax.broadcasted_iota(jnp.int32, (8, PTS), 0)


def coordinate_parts(s):
    row = rows8()
    sq = s * s
    nx = sq[0:1] + sq[1:2] + sq[2:3]
    ny = sq[4:5] + sq[5:6] + sq[6:7]
    full = jnp.where(row == 3, nx, jnp.where(row == 7, ny, s))
    return split3(full)


def source_features(parts):
    p0, p1, p2 = parts
    one = jnp.ones((8, PTS), F32)
    stack = jnp.concatenate([p0, p0, p0, p1, p1, p2, one, one], axis=0)
    return jnp.transpose(stack).astype(BF16)


def target_features(parts):
    p0, p1, p2 = parts
    row = rows8()
    norm = (row == 3) | (row == 7)
    a0 = jnp.where(norm, -1.0, 2.0 * p0)
    a1 = jnp.where(norm, 0.0, 2.0 * p1)
    a2 = jnp.where(norm, 0.0, 2.0 * p2)
    n0 = jnp.where(norm, -p0, 0.0)
    n1 = jnp.where(norm, -p1, 0.0)
    n2 = jnp.where((row == 2) | (row == 6), -pltpu.roll(p2, 7, 0), 0.0)
    stack = jnp.concatenate([a0, a1, a2, a0, a1, a0, n0, n1 + n2], axis=0).astype(BF16)
    top = (lax.broadcasted_iota(jnp.int32, (64, PTS), 0) & 4) == 0
    ones = jnp.where(top, 1.0, 0.0).astype(BF16)
    zeros = jnp.where(top, 0.0, 1.0).astype(BF16)
    return stack * ones, stack * zeros


def moment_features(parts):
    p0, p1, p2 = parts
    row = rows8()
    first = jnp.where(row == 3, 1.0, jnp.where(row > 3, p0, 0.0))
    first = jnp.where(row == 7, 0.0, first)
    second = jnp.where((row > 3) & (row < 7), p1, 0.0) + jnp.where(
        row < 3, pltpu.roll(p2, 4, 0), 0.0
    )
    m = jnp.concatenate([first, second], axis=0).astype(BF16)
    return jnp.concatenate([m, m], axis=1)


def coef_features(minus, neg_dev):
    row = rows8()
    pair = jnp.where(row == 0, minus, jnp.where(row == 1, neg_dev, 0.0))
    h, m, l = split3(pair)
    q = h + pltpu.roll(m, 2, 0) + pltpu.roll(l, 4, 0)
    even = (row == 0) | (row == 2) | (row == 4)
    odd = (row == 1) | (row == 3) | (row == 5)
    src = jnp.transpose(jnp.concatenate([q, jnp.ones((8, PTS), F32)], axis=0)).astype(BF16)
    t0 = jnp.concatenate([jnp.where(even, 1.0, 0.0), jnp.where(even, q, 0.0)], axis=0)
    t1 = jnp.concatenate([jnp.where(odd, 1.0, 0.0), jnp.where(odd, q, 0.0)], axis=0)
    return src, t0.astype(BF16), t1.astype(BF16)


def one_row(c):
    return pl.ds(c, 1)


def loop(n, fn, unroll):
    lax.fori_loop(0, n, lambda c, _: (fn(c), 0)[1], 0, unroll=unroll)


def pack_kernel(edges, x_ref, u_ref, v_ref, bulk, shear, volume, s_out, v_out, mean,
                sc_out, sa_out, vc_out, va_out):
    zero = jnp.zeros((8, PTS), F32)
    s_rows = s_out.reshape(CL * 8, PTS)
    v_rows = v_out.reshape(CL * 8, PTS)

    def eight(i):
        r = pl.ds(pl.multiple_of(i * 8, 8), 8)

        def put(ref, k, value):
            ref[pl.ds(i * 64 + k, 8, stride=8), :] = value

        x = [KAPPA * x_ref[k, r, :] for k in range(3)]
        y = [x[k] + KAPPA * u_ref[k, r, :] for k in range(3)]
        vol = volume[r, :]
        mu = shear[r, :]
        dil = (3.0 * bulk[r, :] - 5.0 * mu) / vol
        dev = 15.0 * mu / vol
        thr = (3.0 / LOG2E) / vol
        v = [KAPPA * v_ref[k, r, :] for k in range(3)]
        for k, value in enumerate([*x, zero, *y, zero]):
            put(s_rows, k, value)
        for k, value in enumerate([dil, dev, thr, zero, *v, zero]):
            put(v_rows, k, value)

    loop(CL // 8, eight, 2)
    total = jnp.sum(jnp.sum(s_out[...], axis=0), axis=1, keepdims=True)
    mean[...] = jnp.broadcast_to(total * (1.0 / OWN), (8, PTS))

    def copy(f):
        for side, s, v in ((0, sc_out, vc_out), (1, sa_out, va_out)):
            e = edges[side, f]
            s[f] = s_out[e]
            v[f] = v_out[e]

    loop(FACING, copy, 4)


def build_one(c, s, left, right, moments):
    parts = coordinate_parts(s)
    if left is not None:
        left[c] = source_features(parts)
    t0, t1 = target_features(parts)
    right[c, :, 0:PTS] = t0
    right[c, :, PTS:] = t1
    moments[c] = moment_features(parts)


def build_kernel(s_own, mean, left, right, moments, token):
    build_own(s_own, mean, left, right, moments)
    token[...] = mean[...]


def build_own(s_own, mean, left, right, moments):
    shift = mean[...]
    loop(CL, lambda c: build_one(c, s_own[c] - shift, left, right, moments), 4)


def build_ghosts(s_c, s_a, mean, right, moments):
    shift = mean[...]

    def ghost(f):
        build_one(CL + f, s_c[f] - shift, None, right, moments)
        build_one(CL + FACING + f, s_a[f] - shift, None, right, moments)

    loop(FACING, ghost, 4)


def ghosts_kernel(s_c, s_a, mean, right_in, moments_in, right, moments):
    build_ghosts(s_c, s_a, mean, right, moments)


def turns_here(counts, grouped):
    if not grouped:
        return 0, (counts[1] + UNROLL - 1) // UNROLL
    first = pl.program_id(0) * GROUP
    return first, jnp.clip((counts[1] - first + UNROLL - 1) // UNROLL, 0, GROUP // UNROLL)


def first_sweep(pairs, counts, grouped, weight_of, left, right, acc, racc):
    first, turns = turns_here(counts, grouped)

    def turn(i, _):
        for j in range(UNROLL):
            k = i * UNROLL + j
            slot = first + k
            p = pairs[0, slot]
            q = pairs[1, slot]
            live = slot < counts[1]
            ab = dot(left[p], right[q], NN)
            na = ab[:, :PTS]
            nb = ab[:, PTS:]
            w = weight_of(na, k, slot)
            x = jnp.maximum(na * nb, TINY)
            t = (x * lax.rsqrt(x) + na) * w
            acc[jnp.where(live, q, EXT)] += jnp.sum(t.reshape(16, 8, PTS), axis=0)
            racc[jnp.where(live, p, CL)] += t
        return 0

    lax.fori_loop(0, turns, turn, 0)


def first_finish(edges, acc, racc, n_own, n_c, n_a, send_c, send_a):
    ones = jnp.ones((2 * PTS, PTS), BF16)
    i0 = lax.broadcasted_iota(jnp.int32, (PTS, PTS), 0)
    i1 = lax.broadcasted_iota(jnp.int32, (PTS, PTS), 1)
    diagonal = i0 == i1

    def own(c):
        h, l = hilo(racc[c])
        across = dot(jnp.concatenate([h, l], axis=1), ones, NN)
        along = jnp.sum(jnp.where(diagonal, across, 0.0).reshape(16, 8, PTS), axis=0)
        n_own[one_row(c), :] = jnp.sum(along + acc[c], axis=0, keepdims=True)

    loop(CL, own, 8)

    def ghost(f):
        r = one_row(f)
        n_c[r, :] = jnp.sum(acc[CL + f], axis=0, keepdims=True)
        n_a[r, :] = jnp.sum(acc[CL + FACING + f], axis=0, keepdims=True)
        send_c[r, :] = n_own[one_row(edges[0, f]), :]
        send_a[r, :] = n_own[one_row(edges[1, f]), :]

    loop(FACING, ghost, 4)


def clear(ref):
    n = ref.shape[0] // 8 * 8
    zero = jnp.zeros(ref.shape[1:], ref.dtype)

    def one(c):
        ref[c] = zero

    loop(n, one, 8)
    for c in range(n, ref.shape[0]):
        one(c)


def dilatation_first(
    pairs, counts, edges, left, right, damage,
    mask_out, n_own, n_c, n_a, send_c, send_a,
    acc, racc, cut,
):
    g = pl.program_id(0)

    @pl.when(g == 0)
    def _():
        clear(acc)
        clear(racc)
        i0 = lax.broadcasted_iota(jnp.int32, (PTS, PTS), 0)
        i1 = lax.broadcasted_iota(jnp.int32, (PTS, PTS), 1)
        cut[0] = jnp.where(i0 < i1, 0, 1)
        cut[1] = jnp.zeros((PTS, PTS), jnp.int32)

    def weight_of(na, k, slot):
        keep = damage[k] > cut[jnp.where(slot < CL, 0, 1)]
        mask_out[slot] = jnp.where(keep, 1.0, 0.0).astype(BF16)
        return jnp.where(keep, jnp.exp2(na), 0.0)

    first_sweep(pairs, counts, True, weight_of, left, right, acc, racc)

    @pl.when(g == pl.num_programs(0) - 1)
    def _():
        first_finish(edges, acc, racc, n_own, n_c, n_a, send_c, send_a)


def advance_kernel(
    edges, s_own, s_c, s_a, v_own, v_c, v_a, mean, f_own, f_c, f_a, up_c, up_a, back_c, back_a,
    s_own2, s_c2, s_a2, v_own2, v_c2, v_a2, left, right, moments,
):
    advance(edges, s_own, s_c, s_a, v_own, v_c, v_a, f_own, f_c, f_a, up_c, up_a, back_c,
            back_a, s_own2, s_c2, s_a2, v_own2, v_c2, v_a2)
    build_own(s_own2, mean, left, right, moments)
    build_ghosts(s_c2, s_a2, mean, right, moments)


def dilatation_again(
    pairs, counts, edges, left, right, mask, n_own, n_c, n_a, send_c, send_a, acc, racc
):
    clear(acc)
    clear(racc)
    weight_of = lambda na, k, slot: mask[slot].astype(F32) * jnp.exp2(na)
    first_sweep(pairs, counts, False, weight_of, left, right, acc, racc)
    first_finish(edges, acc, racc, n_own, n_c, n_a, send_c, send_a)


def advance(edges, s_own, s_c, s_a, v_own, v_c, v_a, f_own, f_c, f_a, up_c, up_a, back_c, back_a,
            s_own2, s_c2, s_a2, v_own2, v_c2, v_a2):
    pad = jnp.zeros((4, PTS), F32)

    def moved(s, v, f):
        v2 = v + TIMESTEP * jnp.concatenate([pad, f], axis=0)
        return s + jnp.where(rows8() < 4, 0.0, TIMESTEP * v2), v2

    def own(c):
        s_own2[c], v_own2[c] = moved(s_own[c], v_own[c], f_own[c])

    loop(CL, own, 8)

    def ghost(f):
        for side, back in ((0, back_c), (1, back_a)):
            e = edges[side, f]
            s_own2[e], v_own2[e] = moved(s_own[e], v_own[e], f_own[e] + back[f])
        s_c2[f], v_c2[f] = moved(s_c[f], v_c[f], up_c[f] + f_c[f])
        s_a2[f], v_a2[f] = moved(s_a[f], v_a[f], up_a[f] + f_a[f])

    loop(FACING, ghost, 4)


def force_pass(
    pairs, counts, edges, left, right, moments, s_own, s_c, s_a, v_own, v_c, v_a, mean,
    n_own, n_c, n_a, up_c, up_a, back_c, back_a, mask,
    theta_out, f_own, f_c, f_a, send_c, send_a,
    left2, right2, acc, n_full, geo, halves,
):
    def geometry(slot, j):
        s = jnp.minimum(slot, SLOTS - 1)
        p = pairs[0, s]
        q = pairs[1, s]
        geo[j, :, 0 : 2 * PTS] = dot(left[p], right[q], NN)
        geo[j, :, 2 * PTS :] = dot(left2[p], right2[q], NN)

    def chain(k, j):
        na = jnp.minimum(geo[j, :, 0:PTS], -TINY)
        nb = jnp.minimum(geo[j, :, PTS : 2 * PTS], -TINY)
        nu = nb - SOFTEN * LOG2E
        za = na * lax.rsqrt(na * nu)
        zb = nb * lax.rsqrt(nb * nu)
        m = jnp.exp2(na) * (geo[j, :, 2 * PTS : 3 * PTS] * za + geo[j, :, 3 * PTS :] * zb)
        h, l = hilo(m)
        keep = mask[k]
        halves[j, 0:PTS, :] = h * keep
        halves[j, PTS:, :] = l * keep

    def gather(slot, j):
        s = jnp.maximum(slot, 0)
        p = pairs[0, s]
        q = pairs[1, s]
        live = (slot >= 0) & (slot < counts[1])
        hl = halves[j]
        gq = dot(moments[p], hl, NN)
        gp = dot(moments[q], jnp.concatenate([hl[:PTS], hl[PTS:]], axis=1), NT)
        return jnp.where(live, p, EXT), jnp.where(live, q, EXT), gp, gq

    def flush(found):
        for pa, qa, gp, gq in found:
            acc[qa] += gq
            acc[pa] += gp

    @pl.when(counts[1] > 0)
    def _():
        clear(acc)
        n_full[0:CL, :] = n_own[...]

        def mend(f):
            r = one_row(f)
            for side, back in ((0, back_c), (1, back_a)):
                e = one_row(edges[side, f])
                n_full[e, :] = n_own[e, :] + back[r, :]
            n_full[one_row(CL + f), :] = up_c[r, :] + n_c[r, :]
            n_full[one_row(CL + FACING + f), :] = up_a[r, :] + n_a[r, :]

        loop(FACING, mend, 4)

        def coefs(c, v):
            theta = v[2:3] * n_full[one_row(c), :]
            src, t0, t1 = coef_features(v[1:2] - v[0:1] * theta, -v[1:2])
            right2[c, :, 0:PTS] = t0
            right2[c, :, PTS:] = t1
            return theta, src

        def own(c):
            theta, src = coefs(c, v_own[c])
            theta_out[one_row(c), :] = theta
            left2[c] = src

        loop(CL, own, 4)

        def ghost(f):
            coefs(CL + f, v_c[f])
            coefs(CL + FACING + f, v_a[f])

        loop(FACING, ghost, 4)
        for j in range(FORCE_UNROLL):
            geometry(j, j)

    def turn(i, _):
        base = i * FORCE_UNROLL
        found = []
        for j in range(FORCE_UNROLL + 1):
            if j < FORCE_UNROLL:
                found.append(gather(base - FORCE_UNROLL + j, j))
            if j > 0:
                chain(base + j - 1, j - 1)
                geometry(base + FORCE_UNROLL + j - 1, j - 1)
        flush(found)
        return 0

    turns = (counts[1] + FORCE_UNROLL - 1) // FORCE_UNROLL
    lax.fori_loop(0, turns, turn, 0)

    @pl.when(counts[1] > 0)
    def _():
        last = (counts[1] + FORCE_UNROLL - 1) // FORCE_UNROLL * FORCE_UNROLL - FORCE_UNROLL
        flush([gather(last + j, j) for j in range(FORCE_UNROLL)])
        shift = mean[...]

        def force(c, s):
            gsum = acc[c]
            first, second = gsum[0:8], gsum[8:16]
            total = first + second + pltpu.roll(second, 4, 0)
            return (total - (s - shift) * first[3:4])[4:8]

        def own(c):
            f_own[c] = force(c, s_own[c])

        loop(CL, own, 4)

        def ghost(f):
            f_c[f] = force(CL + f, s_c[f])
            f_a[f] = force(CL + FACING + f, s_a[f])
            send_c[f] = f_own[edges[0, f]]
            send_a[f] = f_own[edges[1, f]]

        loop(FACING, ghost, 4)


def finish_kernel(edges, u_ref, s_start, s_own, v_own, f_own, back_c, back_a, u_out, vel_out, f_sum):
    f_sum[...] = f_own[...]

    def mend(f):
        for side, back in ((0, back_c), (1, back_a)):
            e = edges[side, f]
            f_sum[e] = f_sum[e] + back[f]

    loop(FACING, mend, 4)

    views = [t.reshape(CL * 8, PTS) for t in (s_own, s_start, v_own)]
    f_rows = f_sum.reshape(CL * 4, PTS)

    def eight(i):
        r = pl.ds(pl.multiple_of(i * 8, 8), 8)
        for k in range(3):
            now, start, vel = (t[pl.ds(i * 64 + 4 + k, 8, stride=8), :] for t in views)
            vel = vel + TIMESTEP * f_rows[pl.ds(i * 32 + k, 8, stride=4), :]
            vel_out[k, r, :] = vel * (1.0 / KAPPA)
            gone = (now - start) + TIMESTEP * vel
            u_out[k, r, :] = u_ref[k, r, :] + gone * (1.0 / KAPPA)

    loop(CL // 8, eight, 2)


SMEM = pl.BlockSpec(memory_space=pltpu.SMEM)
VMEM = pl.BlockSpec(memory_space=pltpu.VMEM)


def table(*shape):
    return jax.ShapeDtypeStruct(shape, F32)


def slab_spec():
    def index(g, pairs, counts):
        return (jnp.minimum(g, (counts[1] - 1) // GROUP), 0, 0)

    return pl.BlockSpec((GROUP, PTS, PTS), index)


def sweep(kernel, name, pairs, counts, edges, tables, out_tables, scratch, damage=None):
    slab = [] if damage is None else [damage]
    return pl.pallas_call(
        kernel,
        out_shape=out_tables,
        grid_spec=pltpu.PrefetchScalarGridSpec(
            num_scalar_prefetch=2,
            grid=(SLOTS // GROUP,) if slab else (1,),
            in_specs=[SMEM] + [VMEM] * len(tables) + [slab_spec()] * len(slab),
            out_specs=[VMEM] * len(out_tables),
            scratch_shapes=scratch,
        ),
        compiler_params=pltpu.CompilerParams(
            dimension_semantics=("arbitrary",), vmem_limit_bytes=KERNEL_VMEM
        ),
        name=name,
    )(pairs, counts, edges, *tables, *slab)


LEFT = jax.ShapeDtypeStruct((CL, PTS, 64), BF16)
RIGHT = jax.ShapeDtypeStruct((EXT, 64, 2 * PTS), BF16)
MOMENTS = jax.ShapeDtypeStruct((EXT, 16, 2 * PTS), BF16)
N_TABLES = [table(CL, PTS)] + [table(FACING, PTS)] * 4
F_TABLES = [table(CL, 4, PTS)] + [table(FACING, 4, PTS)] * 4
STATES = [table(CL, 8, PTS), table(FACING, 8, PTS), table(FACING, 8, PTS)]
SUMS = [pltpu.VMEM((EXT + 1, 8, PTS), F32), pltpu.VMEM((CL + 1, PTS, PTS), F32)]


def small(kernel, name, out_shape, args, smem=0, aliases=None, moved=1 << 20):
    return pl.pallas_call(
        kernel,
        out_shape=out_shape,
        in_specs=[SMEM] * smem + [VMEM] * (len(args) - smem),
        out_specs=[VMEM] * len(out_shape),
        input_output_aliases=aliases or {},
        compiler_params=pltpu.CompilerParams(vmem_limit_bytes=KERNEL_VMEM),
        cost_estimate=pl.CostEstimate(flops=0, bytes_accessed=moved, transcendentals=0),
        name=name,
    )(*args)


def run_build(s_own, mean):
    return small(
        build_kernel, "build", [LEFT, RIGHT, MOMENTS, table(8, PTS)], [s_own, mean], moved=16 << 20
    )


def run_ghosts(s_c, s_a, mean, right, moments):
    return small(
        ghosts_kernel, "ghosts", [RIGHT, MOMENTS], [s_c, s_a, mean, right, moments],
        aliases={3: 0, 4: 1},
    )


def run_advance(edges, tables):
    return small(
        advance_kernel, "advance", STATES * 2 + [LEFT, RIGHT, MOMENTS], [edges, *tables], smem=1
    )


def run_first(pairs, counts, edges, tables, damage):
    return sweep(
        dilatation_first, "dil0", pairs, counts, edges, tables,
        [jax.ShapeDtypeStruct((SLOTS, PTS, PTS), BF16), *N_TABLES],
        [*SUMS, pltpu.VMEM((2, PTS, PTS), jnp.int32)],
        damage,
    )


def run_again(pairs, counts, edges, tables):
    return sweep(dilatation_again, "dil1", pairs, counts, edges, tables, N_TABLES, SUMS)


def run_force(pairs, counts, edges, tables):
    return sweep(
        force_pass, "force", pairs, counts, edges, tables, [table(CL, PTS)] + F_TABLES,
        [
            pltpu.VMEM((CL, PTS, 16), BF16),
            pltpu.VMEM((EXT, 16, 2 * PTS), BF16),
            pltpu.VMEM((EXT + 1, 16, PTS), F32),
            pltpu.VMEM((EXT, PTS), F32),
            pltpu.VMEM((FORCE_UNROLL, PTS, 4 * PTS), F32),
            pltpu.VMEM((FORCE_UNROLL, 2 * PTS, PTS), BF16),
        ],
    )


def run_pack(edges, *args):
    return pl.pallas_call(
        pack_kernel,
        out_shape=[table(CL, 8, PTS)] * 2 + [table(8, PTS)] + [table(FACING, 8, PTS)] * 4,
        in_specs=[SMEM] + [VMEM] * 6,
        out_specs=[VMEM] * 7,
        name="pack",
    )(edges, *args)


def run_finish(edges, *args):
    return pl.pallas_call(
        finish_kernel,
        out_shape=[table(3, CL, PTS), table(3, CL, PTS)],
        in_specs=[SMEM] + [VMEM] * 7,
        out_specs=[VMEM] * 2,
        scratch_shapes=[pltpu.VMEM((CL, 4, PTS), F32)],
        name="finish",
    )(edges, *args)


def shift_ring(block, axis, by):
    n = lax.axis_size(axis)
    return lax.ppermute(block, axis, [(i, (i + by) % n) for i in range(n)])


def exchange(part_c, part_a, own_c, own_a):
    return (
        shift_ring(own_c, "circ", -1),
        shift_ring(own_a, "axial", -1),
        shift_ring(part_c, "circ", 1),
        shift_ring(part_a, "axial", 1),
    )


def body(
    position, displacement, velocity, bulk, shear, volume, edges, block_pairs, block_counts, damage
):
    cube = lambda t: t.reshape(3, CL, PTS)
    flat = lambda t: t.reshape(CL, PTS)
    u = cube(displacement)
    edge = edges[0, 0]
    pairs = block_pairs[0, 0]
    counts = block_counts[0, 0]
    s_own, v_own, mean, s_c, s_a, v_c, v_a = run_pack(
        edge, cube(position), u, cube(velocity), flat(bulk), flat(shear), flat(volume)
    )
    s_start = s_own
    s_c = shift_ring(s_c, "circ", -1)
    s_a = shift_ring(s_a, "axial", -1)
    left, right, moments, token = run_build(s_own, mean)
    v_c, v_a, mean = lax.optimization_barrier((v_c, v_a, token))
    right, moments = run_ghosts(s_c, s_a, mean, right, moments)
    v_c = shift_ring(v_c, "circ", -1)
    v_a = shift_ring(v_a, "axial", -1)
    mask, n_own, n_c, n_a, send_c, send_a = run_first(
        pairs, counts, edge, [left, right], damage[0, 0]
    )
    for step in range(STEPS):
        got = exchange(n_c, n_a, send_c, send_a)
        theta, f_own, f_c, f_a, send_c, send_a = run_force(
            pairs, counts, edge,
            [left, right, moments, s_own, s_c, s_a, v_own, v_c, v_a, mean, n_own, n_c, n_a, *got,
             mask],
        )
        if step == STEPS - 1:
            back_c = shift_ring(f_c, "circ", 1)
            back_a = shift_ring(f_a, "axial", 1)
            u_out, vel_out = run_finish(edge, u, s_start, s_own, v_own, f_own, back_c, back_a)
        else:
            got = exchange(f_c, f_a, send_c, send_a)
            s_own, s_c, s_a, v_own, v_c, v_a, left, right, moments = run_advance(
                edge, [s_own, s_c, s_a, v_own, v_c, v_a, mean, f_own, f_c, f_a, *got]
            )
            n_own, n_c, n_a, send_c, send_a = run_again(
                pairs, counts, edge, [left, right, mask]
            )
    wide = lambda t: t.reshape(3, 1, 1, OWN)
    return wide(u_out), wide(vel_out), theta.reshape(1, 1, OWN)


def solution(mesh):
    placed = (
        P(None, "circ", "axial", None),
        P(None, "circ", "axial", None),
        P(None, "circ", "axial", None),
        P("circ", "axial", None),
        P("circ", "axial", None),
        P("circ", "axial", None),
        P("circ", "axial", None, None),
        P("circ", "axial", None, None),
        P("circ", "axial", None),
        P("circ", "axial", None, None, None),
    )
    return jax.shard_map(
        body,
        mesh=mesh,
        in_specs=placed,
        out_specs=(
            P(None, "circ", "axial", None),
            P(None, "circ", "axial", None),
            P("circ", "axial", None),
        ),
        check_vma=False,
    )
```

```python
import functools

import jax
import jax.numpy as jnp
from jax import lax
from jax.experimental import pallas as pl
from jax.experimental.pallas import tpu as pltpu
from jax.sharding import PartitionSpec as P

PTS = 128
CL = 128
FACING = 32
EXT = CL + 2 * FACING
SLOTS = 320
STEPS = 2
TIMESTEP = 0.07
SOFTEN = 0.01
LOG2E = 1.4426950408889634
KAPPA = LOG2E**0.5
TINY = 1e-30
GROUP = 32
UNROLL = 16
FORCE_UNROLL = 16
KERNEL_VMEM = 21 << 20
OWN = CL * PTS
GHOST = FACING * PTS
F32 = jnp.float32
BF16 = jnp.bfloat16
NT = (((1,), (1,)), ((), ()))
NN = (((1,), (0,)), ((), ()))


def dot(a, b, dims):
    return lax.dot_general(a, b, dims, preferred_element_type=F32)


def split3(x):
    h = x.astype(BF16).astype(F32)
    rest = x - h
    m = rest.astype(BF16).astype(F32)
    return h, m, rest - m


def hilo(x):
    h = x.astype(BF16)
    return h, (x - h.astype(F32)).astype(BF16)


def rows8():
    return lax.broadcasted_iota(jnp.int32, (8, PTS), 0)


def coordinate_parts(s):
    row = rows8()
    sq = s * s
    nx = sq[0:1] + sq[1:2] + sq[2:3]
    ny = sq[4:5] + sq[5:6] + sq[6:7]
    full = jnp.where(row == 3, nx, jnp.where(row == 7, ny, s))
    return split3(full)


def source_features(parts):
    p0, p1, p2 = parts
    one = jnp.ones((8, PTS), F32)
    stack = jnp.concatenate([p0, p0, p0, p1, p1, p2, one, one], axis=0)
    return jnp.transpose(stack).astype(BF16)


def target_features(parts):
    p0, p1, p2 = parts
    row = rows8()
    norm = (row == 3) | (row == 7)
    a0 = jnp.where(norm, -1.0, 2.0 * p0)
    a1 = jnp.where(norm, 0.0, 2.0 * p1)
    a2 = jnp.where(norm, 0.0, 2.0 * p2)
    n0 = jnp.where(norm, -p0, 0.0)
    n1 = jnp.where(norm, -p1, 0.0)
    n2 = jnp.where((row == 2) | (row == 6), -pltpu.roll(p2, 7, 0), 0.0)
    stack = jnp.concatenate([a0, a1, a2, a0, a1, a0, n0, n1 + n2], axis=0).astype(BF16)
    top = (lax.broadcasted_iota(jnp.int32, (64, PTS), 0) & 4) == 0
    ones = jnp.where(top, 1.0, 0.0).astype(BF16)
    zeros = jnp.where(top, 0.0, 1.0).astype(BF16)
    return stack * ones, stack * zeros


def moment_features(parts):
    p0, p1, p2 = parts
    row = rows8()
    first = jnp.where(row == 3, 1.0, jnp.where(row > 3, p0, 0.0))
    first = jnp.where(row == 7, 0.0, first)
    second = jnp.where((row > 3) & (row < 7), p1, 0.0) + jnp.where(
        row < 3, pltpu.roll(p2, 4, 0), 0.0
    )
    m = jnp.concatenate([first, second], axis=0).astype(BF16)
    return jnp.concatenate([m, m], axis=1)


def coef_features(minus, neg_dev):
    row = rows8()
    pair = jnp.where(row == 0, minus, jnp.where(row == 1, neg_dev, 0.0))
    h, m, l = split3(pair)
    q = h + pltpu.roll(m, 2, 0) + pltpu.roll(l, 4, 0)
    even = (row == 0) | (row == 2) | (row == 4)
    odd = (row == 1) | (row == 3) | (row == 5)
    src = jnp.transpose(jnp.concatenate([q, jnp.ones((8, PTS), F32)], axis=0)).astype(BF16)
    stack = jnp.concatenate([jnp.ones((8, PTS), F32), q], axis=0).astype(BF16)
    even2 = jnp.concatenate([jnp.where(even, 1.0, 0.0)] * 2, axis=0).astype(BF16)
    odd2 = jnp.concatenate([jnp.where(odd, 1.0, 0.0)] * 2, axis=0).astype(BF16)
    return src, stack * even2, stack * odd2


def one_row(c):
    return pl.ds(c, 1)


def loop(n, fn, unroll):
    lax.fori_loop(0, n, lambda c, _: (fn(c), 0)[1], 0, unroll=unroll)


def pack_kernel(edges, *refs):
    sources, outs, held, sems = refs[:6], refs[6:13], refs[13:19], refs[19]
    s_out, v_out, mean, sc_out, sa_out, vc_out, va_out = outs
    x_ref, u_ref, v_ref, bulk, shear, volume = held
    copies = [pltpu.make_async_copy(sources[i], held[i], sems.at[i]) for i in range(6)]
    for c in copies:
        c.start()
    for c in copies:
        c.wait()
    zero = jnp.zeros((8, PTS), F32)
    s_rows = s_out.reshape(CL * 8, PTS)
    v_rows = v_out.reshape(CL * 8, PTS)

    def eight(i):
        r = pl.ds(pl.multiple_of(i * 8, 8), 8)

        def put(ref, k, value):
            ref[pl.ds(i * 64 + k, 8, stride=8), :] = value

        x = [KAPPA * x_ref[k, r, :] for k in range(3)]
        y = [x[k] + KAPPA * u_ref[k, r, :] for k in range(3)]
        vol = volume[r, :]
        mu = shear[r, :]
        dil = (3.0 * bulk[r, :] - 5.0 * mu) / vol
        dev = 15.0 * mu / vol
        thr = (3.0 / LOG2E) / vol
        v = [KAPPA * v_ref[k, r, :] for k in range(3)]
        for k, value in enumerate([*x, zero, *y, zero]):
            put(s_rows, k, value)
        for k, value in enumerate([dil, dev, thr, zero, *v, zero]):
            put(v_rows, k, value)

    loop(CL // 8, eight, 2)
    total = jnp.sum(jnp.sum(s_out[...], axis=0), axis=1, keepdims=True)
    mean[...] = jnp.broadcast_to(total * (1.0 / OWN), (8, PTS))

    def copy(f):
        for side, s, v in ((0, sc_out, vc_out), (1, sa_out, va_out)):
            e = edges[side, f]
            s[f] = s_out[e]
            v[f] = v_out[e]

    loop(FACING, copy, 4)


def build_one(c, s, left, right, moments):
    parts = coordinate_parts(s)
    if left is not None:
        left[c] = source_features(parts)
    t0, t1 = target_features(parts)
    right[c, :, 0:PTS] = t0
    right[c, :, PTS:] = t1
    moments[c] = moment_features(parts)


def build_kernel(s_own, mean, left, right, moments, token):
    build_own(s_own, mean, left, right, moments)
    token[...] = mean[...]


def build_own(s_own, mean, left, right, moments):
    shift = mean[...]
    loop(CL, lambda c: build_one(c, s_own[c] - shift, left, right, moments), 8)


def build_ghosts(s_c, s_a, mean, right, moments):
    shift = mean[...]

    def ghost(f):
        build_one(CL + f, s_c[f] - shift, None, right, moments)
        build_one(CL + FACING + f, s_a[f] - shift, None, right, moments)

    loop(FACING, ghost, 4)


def ghosts_kernel(s_c, s_a, mean, right_in, moments_in, right, moments):
    build_ghosts(s_c, s_a, mean, right, moments)


def turns_here(counts, grouped):
    if not grouped:
        return 0, (counts[1] + UNROLL - 1) // UNROLL
    first = pl.program_id(0) * GROUP
    return first, jnp.clip((counts[1] - first + UNROLL - 1) // UNROLL, 0, GROUP // UNROLL)


def first_sweep(pairs, counts, grouped, weight_of, left, right, acc, racc):
    first, turns = turns_here(counts, grouped)

    def bond_terms(p, q, k, slot, own):
        ab = dot(left[p], right[q], NN)
        na = ab[:, :PTS]
        nb = ab[:, PTS:]
        w = weight_of(na, k, slot, own)
        x = jnp.maximum(na * nb, TINY)
        return (x * lax.rsqrt(x) + na) * w

    def own_turn(i, _):
        for j in range(UNROLL):
            k = i * UNROLL + j
            slot = first + k
            t = bond_terms(slot, slot, k, slot, True)
            acc[slot] = jnp.sum(t.reshape(16, 8, PTS), axis=0)
            racc[slot] = t
        return 0

    def turn(i, _):
        for j in range(UNROLL):
            k = i * UNROLL + j
            slot = first + k
            p = pairs[0, slot]
            q = pairs[1, slot]
            live = slot < counts[1]
            t = bond_terms(p, q, k, slot, False)
            acc[jnp.where(live, q, EXT)] += jnp.sum(t.reshape(16, 8, PTS), axis=0)
            racc[jnp.where(live, p, CL)] += t
        return 0

    own_turns = jnp.clip((CL - first) // UNROLL, 0, turns)
    lax.fori_loop(0, own_turns, own_turn, 0)
    lax.fori_loop(own_turns, turns, turn, 0)


def first_finish(edges, acc, racc, n_own, n_c, n_a, send_c, send_a):
    ones = jnp.ones((2 * PTS, PTS), BF16)
    i0 = lax.broadcasted_iota(jnp.int32, (PTS, PTS), 0)
    i1 = lax.broadcasted_iota(jnp.int32, (PTS, PTS), 1)
    diagonal = i0 == i1

    def own(c):
        h, l = hilo(racc[c])
        across = dot(jnp.concatenate([h, l], axis=1), ones, NN)
        along = jnp.sum(jnp.where(diagonal, across, 0.0).reshape(16, 8, PTS), axis=0)
        n_own[one_row(c), :] = jnp.sum(along + acc[c], axis=0, keepdims=True)

    loop(CL, own, 8)

    def ghost(f):
        r = one_row(f)
        n_c[r, :] = jnp.sum(acc[CL + f], axis=0, keepdims=True)
        n_a[r, :] = jnp.sum(acc[CL + FACING + f], axis=0, keepdims=True)
        send_c[r, :] = n_own[one_row(edges[0, f]), :]
        send_a[r, :] = n_own[one_row(edges[1, f]), :]

    loop(FACING, ghost, 4)


def clear(ref, start=0):
    n = (ref.shape[0] - start) // 8 * 8
    zero = jnp.zeros(ref.shape[1:], ref.dtype)

    def one(c):
        ref[start + c] = zero

    loop(n, one, 8)
    for c in range(n, ref.shape[0] - start):
        one(c)


def dilatation_first(
    pairs, counts, edges, left, right, damage,
    mask_out, n_own, n_c, n_a, send_c, send_a,
    acc, racc, above,
):
    g = pl.program_id(0)

    @pl.when(g == 0)
    def _():
        clear(acc, CL)
        i0 = lax.broadcasted_iota(jnp.int32, (PTS, PTS), 0)
        i1 = lax.broadcasted_iota(jnp.int32, (PTS, PTS), 1)
        above[...] = jnp.where(i0 < i1, 0, 1)

    def weight_of(na, k, slot, own):
        keep = damage[k] > (above[...] if own else 0)
        mask_out[slot] = jnp.where(keep, 1.0, 0.0).astype(BF16)
        return jnp.where(keep, jnp.exp2(na), 0.0)

    first_sweep(pairs, counts, True, weight_of, left, right, acc, racc)

    @pl.when(g == pl.num_programs(0) - 1)
    def _():
        first_finish(edges, acc, racc, n_own, n_c, n_a, send_c, send_a)


def dilatation_again(
    pairs, counts, edges, s_own, s_c, s_a, v_own, v_c, v_a, mean, f_own, f_c, f_a,
    up_c, up_a, back_c, back_a, mask,
    s_own2, s_c2, s_a2, v_own2, v_c2, v_a2, left, right, moments,
    n_own, n_c, n_a, send_c, send_a, acc, racc,
):
    clear(acc, CL)
    advance(edges, s_own, s_c, s_a, v_own, v_c, v_a, f_own, f_c, f_a, up_c, up_a, back_c,
            back_a, s_own2, s_c2, s_a2, v_own2, v_c2, v_a2)
    build_own(s_own2, mean, left, right, moments)
    build_ghosts(s_c2, s_a2, mean, right, moments)
    weight_of = lambda na, k, slot, own: mask[slot].astype(F32) * jnp.exp2(na)
    first_sweep(pairs, counts, False, weight_of, left, right, acc, racc)
    first_finish(edges, acc, racc, n_own, n_c, n_a, send_c, send_a)


def advance(edges, s_own, s_c, s_a, v_own, v_c, v_a, f_own, f_c, f_a, up_c, up_a, back_c, back_a,
            s_own2, s_c2, s_a2, v_own2, v_c2, v_a2):
    pad = jnp.zeros((4, PTS), F32)

    def moved(s, v, f):
        v2 = v + TIMESTEP * jnp.concatenate([pad, f], axis=0)
        return s + jnp.where(rows8() < 4, 0.0, TIMESTEP * v2), v2

    def own(c):
        s_own2[c], v_own2[c] = moved(s_own[c], v_own[c], f_own[c])

    loop(CL, own, 8)

    def ghost(f):
        for side, back in ((0, back_c), (1, back_a)):
            e = edges[side, f]
            s_own2[e], v_own2[e] = moved(s_own[e], v_own[e], f_own[e] + back[f])
        s_c2[f], v_c2[f] = moved(s_c[f], v_c[f], up_c[f] + f_c[f])
        s_a2[f], v_a2[f] = moved(s_a[f], v_a[f], up_a[f] + f_a[f])

    loop(FACING, ghost, 4)


def force_pass(
    pairs, counts, edges, left, right, moments, s_own, s_c, s_a, v_own, v_c, v_a, mean,
    n_own, n_c, n_a, up_c, up_a, back_c, back_a, mask,
    theta_out, f_own, f_c, f_a, send_c, send_a,
    left2, right2, acc, n_full, geo, halves,
):
    def geometry(slot, j):
        s = jnp.minimum(slot, SLOTS - 1)
        p = pairs[0, s]
        q = pairs[1, s]
        geo[j, :, 0 : 2 * PTS] = dot(left[p], right[q], NN)
        geo[j, :, 2 * PTS :] = dot(left2[p], right2[q], NN)

    def chain(k, j):
        na = jnp.minimum(geo[j, :, 0:PTS], -TINY)
        nb = jnp.minimum(geo[j, :, PTS : 2 * PTS], -TINY)
        nu = nb - SOFTEN * LOG2E
        za = na * lax.rsqrt(na * nu)
        zb = nb * lax.rsqrt(nb * nu)
        m = jnp.exp2(na) * (geo[j, :, 2 * PTS : 3 * PTS] * za + geo[j, :, 3 * PTS :] * zb)
        h, l = hilo(m)
        keep = mask[k]
        halves[j, 0:PTS, :] = h * keep
        halves[j, PTS:, :] = l * keep

    def gather(slot, j):
        s = jnp.maximum(slot, 0)
        p = pairs[0, s]
        q = pairs[1, s]
        live = (slot >= 0) & (slot < counts[1])
        hl = halves[j]
        gq = dot(moments[p], hl, NN)
        gp = dot(moments[q], jnp.concatenate([hl[:PTS], hl[PTS:]], axis=1), NT)
        return jnp.where(live, p, EXT), jnp.where(live, q, EXT), gp, gq

    def flush(found):
        for pa, qa, gp, gq in found:
            acc[qa] += gq
            acc[pa] += gp

    @pl.when(counts[1] > 0)
    def _():
        clear(acc)
        n_full[0:CL, :] = n_own[...]

        def mend(f):
            r = one_row(f)
            for side, back in ((0, back_c), (1, back_a)):
                e = one_row(edges[side, f])
                n_full[e, :] = n_own[e, :] + back[r, :]
            n_full[one_row(CL + f), :] = up_c[r, :] + n_c[r, :]
            n_full[one_row(CL + FACING + f), :] = up_a[r, :] + n_a[r, :]

        loop(FACING, mend, 4)

        def coefs(c, v):
            theta = v[2:3] * n_full[one_row(c), :]
            src, t0, t1 = coef_features(v[1:2] - v[0:1] * theta, -v[1:2])
            right2[c, :, 0:PTS] = t0
            right2[c, :, PTS:] = t1
            return theta, src

        def own(c):
            theta, src = coefs(c, v_own[c])
            theta_out[one_row(c), :] = theta
            left2[c] = src

        loop(CL, own, 8)

        def ghost(f):
            coefs(CL + f, v_c[f])
            coefs(CL + FACING + f, v_a[f])

        loop(FACING, ghost, 4)
        for j in range(FORCE_UNROLL):
            geometry(j, j)

    def turn(i, _):
        base = i * FORCE_UNROLL
        found = []
        for j in range(FORCE_UNROLL + 1):
            if j < FORCE_UNROLL:
                found.append(gather(base - FORCE_UNROLL + j, j))
            if j > 0:
                chain(base + j - 1, j - 1)
                geometry(base + FORCE_UNROLL + j - 1, j - 1)
        flush(found)
        return 0

    turns = (counts[1] + FORCE_UNROLL - 1) // FORCE_UNROLL
    lax.fori_loop(0, turns, turn, 0)

    @pl.when(counts[1] > 0)
    def _():
        last = (counts[1] + FORCE_UNROLL - 1) // FORCE_UNROLL * FORCE_UNROLL - FORCE_UNROLL
        flush([gather(last + j, j) for j in range(FORCE_UNROLL)])
        shift = mean[...]

        def force(c, s):
            gsum = acc[c]
            first, second = gsum[0:8], gsum[8:16]
            total = first + second + pltpu.roll(second, 4, 0)
            return (total - (s - shift) * first[3:4])[4:8]

        def own(c):
            f_own[c] = force(c, s_own[c])

        loop(CL, own, 4)

        def ghost(f):
            f_c[f] = force(CL + f, s_c[f])
            f_a[f] = force(CL + FACING + f, s_a[f])
            send_c[f] = f_own[edges[0, f]]
            send_a[f] = f_own[edges[1, f]]

        loop(FACING, ghost, 4)


def finish_kernel(edges, u_ref, s_start, s_own, v_own, f_own, back_c, back_a, u_out, vel_out, f_sum):
    f_sum[...] = f_own[...]

    def mend(f):
        for side, back in ((0, back_c), (1, back_a)):
            e = edges[side, f]
            f_sum[e] = f_sum[e] + back[f]

    loop(FACING, mend, 4)

    views = [t.reshape(CL * 8, PTS) for t in (s_own, s_start, v_own)]
    f_rows = f_sum.reshape(CL * 4, PTS)

    def eight(i):
        r = pl.ds(pl.multiple_of(i * 8, 8), 8)
        for k in range(3):
            now, start, vel = (t[pl.ds(i * 64 + 4 + k, 8, stride=8), :] for t in views)
            vel = vel + TIMESTEP * f_rows[pl.ds(i * 32 + k, 8, stride=4), :]
            vel_out[k, r, :] = vel * (1.0 / KAPPA)
            gone = (now - start) + TIMESTEP * vel
            u_out[k, r, :] = u_ref[k, r, :] + gone * (1.0 / KAPPA)

    loop(CL // 8, eight, 2)


SMEM = pl.BlockSpec(memory_space=pltpu.SMEM)
VMEM = pl.BlockSpec(memory_space=pltpu.VMEM)


def table(*shape):
    return jax.ShapeDtypeStruct(shape, F32)


def slab_spec():
    def index(g, pairs, counts):
        return (jnp.minimum(g, (counts[1] - 1) // GROUP), 0, 0)

    return pl.BlockSpec((GROUP, PTS, PTS), index)


def sweep(kernel, name, pairs, counts, edges, tables, out_tables, scratch, damage=None):
    slab = [] if damage is None else [damage]
    return pl.pallas_call(
        kernel,
        out_shape=out_tables,
        grid_spec=pltpu.PrefetchScalarGridSpec(
            num_scalar_prefetch=2,
            grid=(SLOTS // GROUP,) if slab else (1,),
            in_specs=[SMEM] + [VMEM] * len(tables) + [slab_spec()] * len(slab),
            out_specs=[VMEM] * len(out_tables),
            scratch_shapes=scratch,
        ),
        compiler_params=pltpu.CompilerParams(
            dimension_semantics=("arbitrary",), vmem_limit_bytes=KERNEL_VMEM
        ),
        name=name,
    )(pairs, counts, edges, *tables, *slab)


LEFT = jax.ShapeDtypeStruct((CL, PTS, 64), BF16)
RIGHT = jax.ShapeDtypeStruct((EXT, 64, 2 * PTS), BF16)
MOMENTS = jax.ShapeDtypeStruct((EXT, 16, 2 * PTS), BF16)
N_TABLES = [table(CL, PTS)] + [table(FACING, PTS)] * 4
F_TABLES = [table(CL, 4, PTS)] + [table(FACING, 4, PTS)] * 4
STATES = [table(CL, 8, PTS), table(FACING, 8, PTS), table(FACING, 8, PTS)]
SUMS = [pltpu.VMEM((EXT + 1, 8, PTS), F32), pltpu.VMEM((CL + 1, PTS, PTS), F32)]


def small(kernel, name, out_shape, args, smem=0, aliases=None, moved=1 << 20):
    return pl.pallas_call(
        kernel,
        out_shape=out_shape,
        in_specs=[SMEM] * smem + [VMEM] * (len(args) - smem),
        out_specs=[VMEM] * len(out_shape),
        input_output_aliases=aliases or {},
        compiler_params=pltpu.CompilerParams(vmem_limit_bytes=KERNEL_VMEM),
        cost_estimate=pl.CostEstimate(flops=0, bytes_accessed=moved, transcendentals=0),
        name=name,
    )(*args)


def run_build(s_own, mean):
    return small(
        build_kernel, "build", [LEFT, RIGHT, MOMENTS, table(8, PTS)], [s_own, mean], moved=16 << 20
    )


def run_ghosts(s_c, s_a, mean, right, moments):
    return small(
        ghosts_kernel, "ghosts", [RIGHT, MOMENTS], [s_c, s_a, mean, right, moments],
        aliases={3: 0, 4: 1},
    )


def run_first(pairs, counts, edges, tables, damage):
    return sweep(
        dilatation_first, "dil0", pairs, counts, edges, tables,
        [jax.ShapeDtypeStruct((SLOTS, PTS, PTS), BF16), *N_TABLES],
        [*SUMS, pltpu.VMEM((PTS, PTS), jnp.int32)],
        damage,
    )


def run_again(pairs, counts, edges, tables):
    return sweep(
        dilatation_again, "dil1", pairs, counts, edges, tables,
        STATES * 2 + [LEFT, RIGHT, MOMENTS] + N_TABLES, SUMS,
    )


def run_force(pairs, counts, edges, tables):
    return sweep(
        force_pass, "force", pairs, counts, edges, tables, [table(CL, PTS)] + F_TABLES,
        [
            pltpu.VMEM((CL, PTS, 16), BF16),
            pltpu.VMEM((EXT, 16, 2 * PTS), BF16),
            pltpu.VMEM((EXT + 1, 16, PTS), F32),
            pltpu.VMEM((EXT, PTS), F32),
            pltpu.VMEM((FORCE_UNROLL, PTS, 4 * PTS), F32),
            pltpu.VMEM((FORCE_UNROLL, 2 * PTS, PTS), BF16),
        ],
    )


def run_pack(edges, *args):
    return pl.pallas_call(
        pack_kernel,
        out_shape=[table(CL, 8, PTS)] * 2 + [table(8, PTS)] + [table(FACING, 8, PTS)] * 4,
        in_specs=[SMEM] + [pl.BlockSpec(memory_space=pltpu.HBM)] * 6,
        out_specs=[VMEM] * 7,
        scratch_shapes=[pltpu.VMEM((3, CL, PTS), F32)] * 3
        + [pltpu.VMEM((CL, PTS), F32)] * 3
        + [pltpu.SemaphoreType.DMA((6,))],
        compiler_params=pltpu.CompilerParams(vmem_limit_bytes=KERNEL_VMEM),
        name="pack",
    )(edges, *[pltpu.with_memory_space_constraint(t, pltpu.HBM) for t in args])


def run_finish(edges, *args):
    return pl.pallas_call(
        finish_kernel,
        out_shape=[table(3, CL, PTS), table(3, CL, PTS)],
        in_specs=[SMEM] + [VMEM] * 7,
        out_specs=[VMEM] * 2,
        scratch_shapes=[pltpu.VMEM((CL, 4, PTS), F32)],
        compiler_params=pltpu.CompilerParams(vmem_limit_bytes=KERNEL_VMEM),
        name="finish",
    )(edges, *args)


def shift_ring(block, axis, by):
    n = lax.axis_size(axis)
    return lax.ppermute(block, axis, [(i, (i + by) % n) for i in range(n)])


def exchange(part_c, part_a, own_c, own_a):
    return (
        shift_ring(own_c, "circ", -1),
        shift_ring(own_a, "axial", -1),
        shift_ring(part_c, "circ", 1),
        shift_ring(part_a, "axial", 1),
    )


def body(
    position, displacement, velocity, bulk, shear, volume, edges, block_pairs, block_counts, damage
):
    cube = lambda t: t.reshape(3, CL, PTS)
    flat = lambda t: t.reshape(CL, PTS)
    u = cube(displacement)
    edge = edges[0, 0]
    pairs = block_pairs[0, 0]
    counts = block_counts[0, 0]
    s_own, v_own, mean, s_c, s_a, v_c, v_a = run_pack(
        edge, cube(position), u, cube(velocity), flat(bulk), flat(shear), flat(volume)
    )
    s_start = s_own
    s_c = shift_ring(s_c, "circ", -1)
    s_a = shift_ring(s_a, "axial", -1)
    left, right, moments, token = run_build(s_own, mean)
    v_c, v_a, mean = lax.optimization_barrier((v_c, v_a, token))
    right, moments = run_ghosts(s_c, s_a, mean, right, moments)
    v_c = shift_ring(v_c, "circ", -1)
    v_a = shift_ring(v_a, "axial", -1)
    mask, n_own, n_c, n_a, send_c, send_a = run_first(
        pairs, counts, edge, [left, right], damage[0, 0]
    )
    for step in range(STEPS):
        got = exchange(n_c, n_a, send_c, send_a)
        theta, f_own, f_c, f_a, send_c, send_a = run_force(
            pairs, counts, edge,
            [left, right, moments, s_own, s_c, s_a, v_own, v_c, v_a, mean, n_own, n_c, n_a, *got,
             mask],
        )
        if step == STEPS - 1:
            back_c = shift_ring(f_c, "circ", 1)
            back_a = shift_ring(f_a, "axial", 1)
            u_out, vel_out = run_finish(edge, u, s_start, s_own, v_own, f_own, back_c, back_a)
        else:
            got = exchange(f_c, f_a, send_c, send_a)
            (s_own, s_c, s_a, v_own, v_c, v_a, left, right, moments, n_own, n_c, n_a, send_c,
             send_a) = run_again(
                pairs, counts, edge,
                [s_own, s_c, s_a, v_own, v_c, v_a, mean, f_own, f_c, f_a, *got, mask],
            )
    wide = lambda t: t.reshape(3, 1, 1, OWN)
    return wide(u_out), wide(vel_out), theta.reshape(1, 1, OWN)


def solution(mesh):
    placed = (
        P(None, "circ", "axial", None),
        P(None, "circ", "axial", None),
        P(None, "circ", "axial", None),
        P("circ", "axial", None),
        P("circ", "axial", None),
        P("circ", "axial", None),
        P("circ", "axial", None, None),
        P("circ", "axial", None, None),
        P("circ", "axial", None),
        P("circ", "axial", None, None, None),
    )
    return jax.shard_map(
        body,
        mesh=mesh,
        in_specs=placed,
        out_specs=(
            P(None, "circ", "axial", None),
            P(None, "circ", "axial", None),
            P("circ", "axial", None),
        ),
        check_vma=False,
    )
```

```python
import functools

import jax
import jax.numpy as jnp
from jax import lax
from jax.experimental import pallas as pl
from jax.experimental.pallas import tpu as pltpu
from jax.sharding import PartitionSpec as P

PTS = 128
CL = 128
FACING = 32
EXT = CL + 2 * FACING
SLOTS = 320
STEPS = 2
TIMESTEP = 0.07
SOFTEN = 0.01
LOG2E = 1.4426950408889634
KAPPA = LOG2E**0.5
TINY = 1e-30
GROUP = 64
UNROLL = 16
FORCE_UNROLL = 20
KERNEL_VMEM = 21 << 20
OWN = CL * PTS
GHOST = FACING * PTS
F32 = jnp.float32
BF16 = jnp.bfloat16
NT = (((1,), (1,)), ((), ()))
NN = (((1,), (0,)), ((), ()))


def dot(a, b, dims):
    return lax.dot_general(a, b, dims, preferred_element_type=F32)


def split3(x):
    h = x.astype(BF16).astype(F32)
    rest = x - h
    m = rest.astype(BF16).astype(F32)
    return h, m, rest - m


def hilo(x):
    h = x.astype(BF16)
    return h, (x - h.astype(F32)).astype(BF16)


def rows8():
    return lax.broadcasted_iota(jnp.int32, (8, PTS), 0)


def coordinate_parts(s):
    row = rows8()
    sq = s * s
    nx = sq[0:1] + sq[1:2] + sq[2:3]
    ny = sq[4:5] + sq[5:6] + sq[6:7]
    full = jnp.where(row == 3, nx, jnp.where(row == 7, ny, s))
    return split3(full)


def source_features(parts):
    p0, p1, p2 = parts
    one = jnp.ones((8, PTS), F32)
    stack = jnp.concatenate([p0, p0, p0, p1, p1, p2, one, one], axis=0)
    return jnp.transpose(stack).astype(BF16)


def target_features(parts):
    p0, p1, p2 = parts
    row = rows8()
    norm = (row == 3) | (row == 7)
    a0 = jnp.where(norm, -1.0, 2.0 * p0)
    a1 = jnp.where(norm, 0.0, 2.0 * p1)
    a2 = jnp.where(norm, 0.0, 2.0 * p2)
    n0 = jnp.where(norm, -p0, 0.0)
    n1 = jnp.where(norm, -p1, 0.0)
    n2 = jnp.where((row == 2) | (row == 6), -pltpu.roll(p2, 7, 0), 0.0)
    stack = jnp.concatenate([a0, a1, a2, a0, a1, a0, n0, n1 + n2], axis=0).astype(BF16)
    top = (lax.broadcasted_iota(jnp.int32, (64, PTS), 0) & 4) == 0
    ones = jnp.where(top, 1.0, 0.0).astype(BF16)
    zeros = jnp.where(top, 0.0, 1.0).astype(BF16)
    return stack * ones, stack * zeros


def moment_features(parts):
    p0, p1, p2 = parts
    row = rows8()
    first = jnp.where(row == 3, 1.0, jnp.where(row > 3, p0, 0.0))
    first = jnp.where(row == 7, 0.0, first)
    second = jnp.where((row > 3) & (row < 7), p1, 0.0) + jnp.where(
        row < 3, pltpu.roll(p2, 4, 0), 0.0
    )
    m = jnp.concatenate([first, second], axis=0).astype(BF16)
    return jnp.concatenate([m, m], axis=1)


def coef_features(minus, neg_dev):
    row = rows8()
    pair = jnp.where(row == 0, minus, jnp.where(row == 1, neg_dev, 0.0))
    h, m, l = split3(pair)
    q = h + pltpu.roll(m, 2, 0) + pltpu.roll(l, 4, 0)
    even = (row == 0) | (row == 2) | (row == 4)
    odd = (row == 1) | (row == 3) | (row == 5)
    src = jnp.transpose(jnp.concatenate([q, jnp.ones((8, PTS), F32)], axis=0)).astype(BF16)
    stack = jnp.concatenate([jnp.ones((8, PTS), F32), q], axis=0).astype(BF16)
    even2 = jnp.concatenate([jnp.where(even, 1.0, 0.0)] * 2, axis=0).astype(BF16)
    odd2 = jnp.concatenate([jnp.where(odd, 1.0, 0.0)] * 2, axis=0).astype(BF16)
    return src, stack * even2, stack * odd2


def one_row(c):
    return pl.ds(c, 1)


def loop(n, fn, unroll):
    lax.fori_loop(0, n, lambda c, _: (fn(c), 0)[1], 0, unroll=unroll)


def pack_kernel(edges, *refs):
    sources, outs, held, sems = refs[:6], refs[6:13], refs[13:19], refs[19]
    s_out, v_out, mean, sc_out, sa_out, vc_out, va_out = outs
    x_ref, u_ref, v_ref, bulk, shear, volume = held
    copies = [pltpu.make_async_copy(sources[i], held[i], sems.at[i]) for i in range(6)]
    for c in copies:
        c.start()
    for c in copies:
        c.wait()
    zero = jnp.zeros((8, PTS), F32)
    s_rows = s_out.reshape(CL * 8, PTS)
    v_rows = v_out.reshape(CL * 8, PTS)

    def eight(i):
        r = pl.ds(pl.multiple_of(i * 8, 8), 8)

        def put(ref, k, value):
            ref[pl.ds(i * 64 + k, 8, stride=8), :] = value

        x = [KAPPA * x_ref[k, r, :] for k in range(3)]
        y = [x[k] + KAPPA * u_ref[k, r, :] for k in range(3)]
        vol = volume[r, :]
        mu = shear[r, :]
        dil = (3.0 * bulk[r, :] - 5.0 * mu) / vol
        dev = 15.0 * mu / vol
        thr = (3.0 / LOG2E) / vol
        v = [KAPPA * v_ref[k, r, :] for k in range(3)]
        for k, value in enumerate([*x, zero, *y, zero]):
            put(s_rows, k, value)
        for k, value in enumerate([dil, dev, thr, zero, *v, zero]):
            put(v_rows, k, value)

    loop(CL // 8, eight, 2)
    total = jnp.sum(jnp.sum(s_out[...], axis=0), axis=1, keepdims=True)
    mean[...] = jnp.broadcast_to(total * (1.0 / OWN), (8, PTS))

    def copy(f):
        for side, s, v in ((0, sc_out, vc_out), (1, sa_out, va_out)):
            e = edges[side, f]
            s[f] = s_out[e]
            v[f] = v_out[e]

    loop(FACING, copy, 4)


def build_one(c, s, left, right, moments):
    parts = coordinate_parts(s)
    if left is not None:
        left[c] = source_features(parts)
    t0, t1 = target_features(parts)
    right[c, :, 0:PTS] = t0
    right[c, :, PTS:] = t1
    moments[c] = moment_features(parts)


def build_kernel(s_own, mean, left, right, moments, token):
    build_own(s_own, mean, left, right, moments)
    token[...] = mean[...]


def build_own(s_own, mean, left, right, moments):
    shift = mean[...]
    loop(CL, lambda c: build_one(c, s_own[c] - shift, left, right, moments), 8)


def build_ghosts(s_c, s_a, mean, right, moments):
    shift = mean[...]

    def ghost(f):
        build_one(CL + f, s_c[f] - shift, None, right, moments)
        build_one(CL + FACING + f, s_a[f] - shift, None, right, moments)

    loop(FACING, ghost, 4)


def ghosts_kernel(s_c, s_a, mean, right_in, moments_in, right, moments):
    build_ghosts(s_c, s_a, mean, right, moments)


def turns_here(counts, grouped):
    if not grouped:
        return 0, (counts[1] + UNROLL - 1) // UNROLL
    first = pl.program_id(0) * GROUP
    return first, jnp.clip((counts[1] - first + UNROLL - 1) // UNROLL, 0, GROUP // UNROLL)


def first_sweep(pairs, counts, grouped, weight_of, left, right, acc, racc):
    first, turns = turns_here(counts, grouped)

    def bond_terms(p, q, k, slot, own):
        ab = dot(left[p], right[q], NN)
        na = ab[:, :PTS]
        nb = ab[:, PTS:]
        w = weight_of(na, k, slot, own)
        x = jnp.maximum(na * nb, TINY)
        return (x * lax.rsqrt(x) + na) * w

    def own_turn(i, _):
        for j in range(UNROLL):
            k = i * UNROLL + j
            slot = first + k
            t = bond_terms(slot, slot, k, slot, True)
            acc[slot] = jnp.sum(t.reshape(16, 8, PTS), axis=0)
            racc[slot] = t
        return 0

    def turn(i, _):
        for j in range(UNROLL):
            k = i * UNROLL + j
            slot = first + k
            p = pairs[0, slot]
            q = pairs[1, slot]
            live = slot < counts[1]
            t = bond_terms(p, q, k, slot, False)
            acc[jnp.where(live, q, EXT)] += jnp.sum(t.reshape(16, 8, PTS), axis=0)
            racc[jnp.where(live, p, CL)] += t
        return 0

    own_turns = jnp.clip((CL - first) // UNROLL, 0, turns)
    lax.fori_loop(0, own_turns, own_turn, 0)
    lax.fori_loop(own_turns, turns, turn, 0)


def first_finish(edges, acc, racc, n_own, n_c, n_a, send_c, send_a):
    ones = jnp.ones((2 * PTS, PTS), BF16)
    i0 = lax.broadcasted_iota(jnp.int32, (PTS, PTS), 0)
    i1 = lax.broadcasted_iota(jnp.int32, (PTS, PTS), 1)
    diagonal = i0 == i1

    def own(c):
        h, l = hilo(racc[c])
        across = dot(jnp.concatenate([h, l], axis=1), ones, NN)
        along = jnp.sum(jnp.where(diagonal, across, 0.0).reshape(16, 8, PTS), axis=0)
        n_own[one_row(c), :] = jnp.sum(along + acc[c], axis=0, keepdims=True)

    loop(CL, own, 8)

    def ghost(f):
        r = one_row(f)
        n_c[r, :] = jnp.sum(acc[CL + f], axis=0, keepdims=True)
        n_a[r, :] = jnp.sum(acc[CL + FACING + f], axis=0, keepdims=True)
        send_c[r, :] = n_own[one_row(edges[0, f]), :]
        send_a[r, :] = n_own[one_row(edges[1, f]), :]

    loop(FACING, ghost, 4)


def clear(ref, start=0):
    n = (ref.shape[0] - start) // 8 * 8
    zero = jnp.zeros(ref.shape[1:], ref.dtype)

    def one(c):
        ref[start + c] = zero

    loop(n, one, 8)
    for c in range(n, ref.shape[0] - start):
        one(c)


def dilatation_first(
    pairs, counts, edges, left, right, damage,
    mask_out, n_own, n_c, n_a, send_c, send_a,
    acc, racc, above,
):
    g = pl.program_id(0)

    @pl.when(g == 0)
    def _():
        clear(acc, CL)
        i0 = lax.broadcasted_iota(jnp.int32, (PTS, PTS), 0)
        i1 = lax.broadcasted_iota(jnp.int32, (PTS, PTS), 1)
        above[...] = jnp.where(i0 < i1, 0, 1)

    def weight_of(na, k, slot, own):
        keep = damage[k] > (above[...] if own else 0)
        mask_out[slot] = jnp.where(keep, 1.0, 0.0).astype(BF16)
        return jnp.where(keep, jnp.exp2(na), 0.0)

    first_sweep(pairs, counts, True, weight_of, left, right, acc, racc)

    @pl.when(g == pl.num_programs(0) - 1)
    def _():
        first_finish(edges, acc, racc, n_own, n_c, n_a, send_c, send_a)


def dilatation_again(
    pairs, counts, edges, s_own, s_c, s_a, v_own, v_c, v_a, mean, f_own, f_c, f_a,
    up_c, up_a, back_c, back_a, mask,
    s_own2, s_c2, s_a2, v_own2, v_c2, v_a2, left, right, moments,
    n_own, n_c, n_a, send_c, send_a, acc, racc,
):
    clear(acc, CL)
    advance(edges, s_own, s_c, s_a, v_own, v_c, v_a, f_own, f_c, f_a, up_c, up_a, back_c,
            back_a, s_own2, s_c2, s_a2, v_own2, v_c2, v_a2)
    build_own(s_own2, mean, left, right, moments)
    build_ghosts(s_c2, s_a2, mean, right, moments)
    weight_of = lambda na, k, slot, own: mask[slot].astype(F32) * jnp.exp2(na)
    first_sweep(pairs, counts, False, weight_of, left, right, acc, racc)
    first_finish(edges, acc, racc, n_own, n_c, n_a, send_c, send_a)


def advance(edges, s_own, s_c, s_a, v_own, v_c, v_a, f_own, f_c, f_a, up_c, up_a, back_c, back_a,
            s_own2, s_c2, s_a2, v_own2, v_c2, v_a2):
    pad = jnp.zeros((4, PTS), F32)

    def moved(s, v, f):
        v2 = v + TIMESTEP * jnp.concatenate([pad, f], axis=0)
        return s + jnp.where(rows8() < 4, 0.0, TIMESTEP * v2), v2

    def own(c):
        s_own2[c], v_own2[c] = moved(s_own[c], v_own[c], f_own[c])

    loop(CL, own, 8)

    def ghost(f):
        for side, back in ((0, back_c), (1, back_a)):
            e = edges[side, f]
            s_own2[e], v_own2[e] = moved(s_own[e], v_own[e], f_own[e] + back[f])
        s_c2[f], v_c2[f] = moved(s_c[f], v_c[f], up_c[f] + f_c[f])
        s_a2[f], v_a2[f] = moved(s_a[f], v_a[f], up_a[f] + f_a[f])

    loop(FACING, ghost, 4)


def force_pass(
    pairs, counts, edges, left, right, moments, s_own, s_c, s_a, v_own, v_c, v_a, mean,
    n_own, n_c, n_a, up_c, up_a, back_c, back_a, mask,
    theta_out, f_own, f_c, f_a, send_c, send_a,
    left2, right2, acc, n_full, geo, halves,
):
    def geometry(slot, j):
        s = jnp.minimum(slot, SLOTS - 1)
        p = pairs[0, s]
        q = pairs[1, s]
        geo[j, :, 0 : 2 * PTS] = dot(left[p], right[q], NN)
        geo[j, :, 2 * PTS :] = dot(left2[p], right2[q], NN)

    def chain(k, j):
        na = jnp.minimum(geo[j, :, 0:PTS], -TINY)
        nb = jnp.minimum(geo[j, :, PTS : 2 * PTS], -TINY)
        nu = nb - SOFTEN * LOG2E
        za = na * lax.rsqrt(na * nu)
        zb = nb * lax.rsqrt(nb * nu)
        m = jnp.exp2(na) * (geo[j, :, 2 * PTS : 3 * PTS] * za + geo[j, :, 3 * PTS :] * zb)
        h, l = hilo(m)
        keep = mask[k]
        halves[j, 0:PTS, :] = h * keep
        halves[j, PTS:, :] = l * keep

    def gather(slot, j):
        s = jnp.maximum(slot, 0)
        p = pairs[0, s]
        q = pairs[1, s]
        live = (slot >= 0) & (slot < counts[1])
        hl = halves[j]
        gq = dot(moments[p], hl, NN)
        gp = dot(moments[q], jnp.concatenate([hl[:PTS], hl[PTS:]], axis=1), NT)
        return jnp.where(live, p, EXT), jnp.where(live, q, EXT), gp, gq

    def flush(found):
        for pa, qa, gp, gq in found:
            acc[qa] += gq
            acc[pa] += gp

    @pl.when(counts[1] > 0)
    def _():
        clear(acc)
        n_full[0:CL, :] = n_own[...]

        def mend(f):
            r = one_row(f)
            for side, back in ((0, back_c), (1, back_a)):
                e = one_row(edges[side, f])
                n_full[e, :] = n_own[e, :] + back[r, :]
            n_full[one_row(CL + f), :] = up_c[r, :] + n_c[r, :]
            n_full[one_row(CL + FACING + f), :] = up_a[r, :] + n_a[r, :]

        loop(FACING, mend, 4)

        def coefs(c, v):
            theta = v[2:3] * n_full[one_row(c), :]
            src, t0, t1 = coef_features(v[1:2] - v[0:1] * theta, -v[1:2])
            right2[c, :, 0:PTS] = t0
            right2[c, :, PTS:] = t1
            return theta, src

        def own(c):
            theta, src = coefs(c, v_own[c])
            theta_out[one_row(c), :] = theta
            left2[c] = src

        loop(CL, own, 8)

        def ghost(f):
            coefs(CL + f, v_c[f])
            coefs(CL + FACING + f, v_a[f])

        loop(FACING, ghost, 4)
        for j in range(FORCE_UNROLL):
            geometry(j, j)

    def turn(i, _):
        base = i * FORCE_UNROLL
        found = []
        for j in range(FORCE_UNROLL + 1):
            if j < FORCE_UNROLL:
                found.append(gather(base - FORCE_UNROLL + j, j))
            if j > 0:
                chain(base + j - 1, j - 1)
                geometry(base + FORCE_UNROLL + j - 1, j - 1)
        flush(found)
        return 0

    turns = (counts[1] + FORCE_UNROLL - 1) // FORCE_UNROLL
    lax.fori_loop(0, turns, turn, 0)

    @pl.when(counts[1] > 0)
    def _():
        last = (counts[1] + FORCE_UNROLL - 1) // FORCE_UNROLL * FORCE_UNROLL - FORCE_UNROLL
        flush([gather(last + j, j) for j in range(FORCE_UNROLL)])
        shift = mean[...]

        def force(c, s):
            gsum = acc[c]
            first, second = gsum[0:8], gsum[8:16]
            total = first + second + pltpu.roll(second, 4, 0)
            return (total - (s - shift) * first[3:4])[4:8]

        def own(c):
            f_own[c] = force(c, s_own[c])

        loop(CL, own, 4)

        def ghost(f):
            f_c[f] = force(CL + f, s_c[f])
            f_a[f] = force(CL + FACING + f, s_a[f])
            send_c[f] = f_own[edges[0, f]]
            send_a[f] = f_own[edges[1, f]]

        loop(FACING, ghost, 4)


def finish_kernel(edges, u_ref, s_start, s_own, v_own, f_own, back_c, back_a, u_out, vel_out, f_sum):
    f_sum[...] = f_own[...]

    def mend(f):
        for side, back in ((0, back_c), (1, back_a)):
            e = edges[side, f]
            f_sum[e] = f_sum[e] + back[f]

    loop(FACING, mend, 4)

    views = [t.reshape(CL * 8, PTS) for t in (s_own, s_start, v_own)]
    f_rows = f_sum.reshape(CL * 4, PTS)

    def eight(i):
        r = pl.ds(pl.multiple_of(i * 8, 8), 8)
        for k in range(3):
            now, start, vel = (t[pl.ds(i * 64 + 4 + k, 8, stride=8), :] for t in views)
            vel = vel + TIMESTEP * f_rows[pl.ds(i * 32 + k, 8, stride=4), :]
            vel_out[k, r, :] = vel * (1.0 / KAPPA)
            gone = (now - start) + TIMESTEP * vel
            u_out[k, r, :] = u_ref[k, r, :] + gone * (1.0 / KAPPA)

    loop(CL // 8, eight, 2)


SMEM = pl.BlockSpec(memory_space=pltpu.SMEM)
VMEM = pl.BlockSpec(memory_space=pltpu.VMEM)


def table(*shape):
    return jax.ShapeDtypeStruct(shape, F32)


def slab_spec():
    def index(g, pairs, counts):
        return (jnp.minimum(g, (counts[1] - 1) // GROUP), 0, 0)

    return pl.BlockSpec((GROUP, PTS, PTS), index)


def sweep(kernel, name, pairs, counts, edges, tables, out_tables, scratch, damage=None):
    slab = [] if damage is None else [damage]
    return pl.pallas_call(
        kernel,
        out_shape=out_tables,
        grid_spec=pltpu.PrefetchScalarGridSpec(
            num_scalar_prefetch=2,
            grid=(SLOTS // GROUP,) if slab else (1,),
            in_specs=[SMEM] + [VMEM] * len(tables) + [slab_spec()] * len(slab),
            out_specs=[VMEM] * len(out_tables),
            scratch_shapes=scratch,
        ),
        compiler_params=pltpu.CompilerParams(
            dimension_semantics=("arbitrary",), vmem_limit_bytes=KERNEL_VMEM
        ),
        name=name,
    )(pairs, counts, edges, *tables, *slab)


LEFT = jax.ShapeDtypeStruct((CL, PTS, 64), BF16)
RIGHT = jax.ShapeDtypeStruct((EXT, 64, 2 * PTS), BF16)
MOMENTS = jax.ShapeDtypeStruct((EXT, 16, 2 * PTS), BF16)
N_TABLES = [table(CL, PTS)] + [table(FACING, PTS)] * 4
F_TABLES = [table(CL, 4, PTS)] + [table(FACING, 4, PTS)] * 4
STATES = [table(CL, 8, PTS), table(FACING, 8, PTS), table(FACING, 8, PTS)]
SUMS = [pltpu.VMEM((EXT + 1, 8, PTS), F32), pltpu.VMEM((CL + 1, PTS, PTS), F32)]


def small(kernel, name, out_shape, args, smem=0, aliases=None, moved=1 << 20):
    return pl.pallas_call(
        kernel,
        out_shape=out_shape,
        in_specs=[SMEM] * smem + [VMEM] * (len(args) - smem),
        out_specs=[VMEM] * len(out_shape),
        input_output_aliases=aliases or {},
        compiler_params=pltpu.CompilerParams(vmem_limit_bytes=KERNEL_VMEM),
        cost_estimate=pl.CostEstimate(flops=0, bytes_accessed=moved, transcendentals=0),
        name=name,
    )(*args)


def run_build(s_own, mean):
    return small(
        build_kernel, "build", [LEFT, RIGHT, MOMENTS, table(8, PTS)], [s_own, mean], moved=16 << 20
    )


def run_ghosts(s_c, s_a, mean, right, moments):
    return small(
        ghosts_kernel, "ghosts", [RIGHT, MOMENTS], [s_c, s_a, mean, right, moments],
        aliases={3: 0, 4: 1},
    )


def run_first(pairs, counts, edges, tables, damage):
    return sweep(
        dilatation_first, "dil0", pairs, counts, edges, tables,
        [jax.ShapeDtypeStruct((SLOTS, PTS, PTS), BF16), *N_TABLES],
        [*SUMS, pltpu.VMEM((PTS, PTS), jnp.int32)],
        damage,
    )


def run_again(pairs, counts, edges, tables):
    return sweep(
        dilatation_again, "dil1", pairs, counts, edges, tables,
        STATES * 2 + [LEFT, RIGHT, MOMENTS] + N_TABLES, SUMS,
    )


def run_force(pairs, counts, edges, tables):
    return sweep(
        force_pass, "force", pairs, counts, edges, tables, [table(CL, PTS)] + F_TABLES,
        [
            pltpu.VMEM((CL, PTS, 16), BF16),
            pltpu.VMEM((EXT, 16, 2 * PTS), BF16),
            pltpu.VMEM((EXT + 1, 16, PTS), F32),
            pltpu.VMEM((EXT, PTS), F32),
            pltpu.VMEM((FORCE_UNROLL, PTS, 4 * PTS), F32),
            pltpu.VMEM((FORCE_UNROLL, 2 * PTS, PTS), BF16),
        ],
    )


def run_pack(edges, *args):
    return pl.pallas_call(
        pack_kernel,
        out_shape=[table(CL, 8, PTS)] * 2 + [table(8, PTS)] + [table(FACING, 8, PTS)] * 4,
        in_specs=[SMEM] + [pl.BlockSpec(memory_space=pltpu.HBM)] * 6,
        out_specs=[VMEM] * 7,
        scratch_shapes=[pltpu.VMEM((3, CL, PTS), F32)] * 3
        + [pltpu.VMEM((CL, PTS), F32)] * 3
        + [pltpu.SemaphoreType.DMA((6,))],
        compiler_params=pltpu.CompilerParams(vmem_limit_bytes=KERNEL_VMEM),
        name="pack",
    )(edges, *[pltpu.with_memory_space_constraint(t, pltpu.HBM) for t in args])


def run_finish(edges, *args):
    return pl.pallas_call(
        finish_kernel,
        out_shape=[table(3, CL, PTS), table(3, CL, PTS)],
        in_specs=[SMEM] + [VMEM] * 7,
        out_specs=[VMEM] * 2,
        scratch_shapes=[pltpu.VMEM((CL, 4, PTS), F32)],
        compiler_params=pltpu.CompilerParams(vmem_limit_bytes=KERNEL_VMEM),
        name="finish",
    )(edges, *args)


def shift_ring(block, axis, by):
    n = lax.axis_size(axis)
    return lax.ppermute(block, axis, [(i, (i + by) % n) for i in range(n)])


def exchange(part_c, part_a, own_c, own_a):
    return (
        shift_ring(own_c, "circ", -1),
        shift_ring(own_a, "axial", -1),
        shift_ring(part_c, "circ", 1),
        shift_ring(part_a, "axial", 1),
    )


def body(
    position, displacement, velocity, bulk, shear, volume, edges, block_pairs, block_counts, damage
):
    cube = lambda t: t.reshape(3, CL, PTS)
    flat = lambda t: t.reshape(CL, PTS)
    u = cube(displacement)
    edge = edges[0, 0]
    pairs = block_pairs[0, 0]
    counts = block_counts[0, 0]
    s_own, v_own, mean, s_c, s_a, v_c, v_a = run_pack(
        edge, cube(position), u, cube(velocity), flat(bulk), flat(shear), flat(volume)
    )
    s_start = s_own
    s_c = shift_ring(s_c, "circ", -1)
    s_a = shift_ring(s_a, "axial", -1)
    left, right, moments, token = run_build(s_own, mean)
    v_c, v_a, mean = lax.optimization_barrier((v_c, v_a, token))
    right, moments = run_ghosts(s_c, s_a, mean, right, moments)
    v_c = shift_ring(v_c, "circ", -1)
    v_a = shift_ring(v_a, "axial", -1)
    mask, n_own, n_c, n_a, send_c, send_a = run_first(
        pairs, counts, edge, [left, right], damage[0, 0]
    )
    for step in range(STEPS):
        got = exchange(n_c, n_a, send_c, send_a)
        theta, f_own, f_c, f_a, send_c, send_a = run_force(
            pairs, counts, edge,
            [left, right, moments, s_own, s_c, s_a, v_own, v_c, v_a, mean, n_own, n_c, n_a, *got,
             mask],
        )
        if step == STEPS - 1:
            back_c = shift_ring(f_c, "circ", 1)
            back_a = shift_ring(f_a, "axial", 1)
            u_out, vel_out = run_finish(edge, u, s_start, s_own, v_own, f_own, back_c, back_a)
        else:
            got = exchange(f_c, f_a, send_c, send_a)
            (s_own, s_c, s_a, v_own, v_c, v_a, left, right, moments, n_own, n_c, n_a, send_c,
             send_a) = run_again(
                pairs, counts, edge,
                [s_own, s_c, s_a, v_own, v_c, v_a, mean, f_own, f_c, f_a, *got, mask],
            )
    wide = lambda t: t.reshape(3, 1, 1, OWN)
    return wide(u_out), wide(vel_out), theta.reshape(1, 1, OWN)


def solution(mesh):
    placed = (
        P(None, "circ", "axial", None),
        P(None, "circ", "axial", None),
        P(None, "circ", "axial", None),
        P("circ", "axial", None),
        P("circ", "axial", None),
        P("circ", "axial", None),
        P("circ", "axial", None, None),
        P("circ", "axial", None, None),
        P("circ", "axial", None),
        P("circ", "axial", None, None, None),
    )
    return jax.shard_map(
        body,
        mesh=mesh,
        in_specs=placed,
        out_specs=(
            P(None, "circ", "axial", None),
            P(None, "circ", "axial", None),
            P("circ", "axial", None),
        ),
        check_vma=False,
    )
```
